256 devices in a mesh: dp: 4 (over x), expert: 64 (over z, y, core).
Axes of the slice: x: 4, y: 4, z: 8, core: 2. Of those that a mesh axis runs over, the one named last changes fastest.
Arguments:
- queries: bfloat16 [16384, 2048], P('expert', 'dp'), may hold values from -160 to 160
- kv_pool: bfloat16 [2, 1024, 64, 2048], P(None, 'expert', None, 'dp'), may hold values from -6 to 6
- page_table: int32 [256, 4], P('expert'), may hold values from 0 to 1023, as said below
- ctx_lens: int32 [16384], P('expert'), may hold values from 2 to 256, as said below
- w_out: bfloat16 [2048, 2048], P('dp', 'expert'), may hold values from -0.59765625 to 0.59765625
- residual: bfloat16 [16384, 2048], P(('expert', 'dp')), may hold values from -3 to 3
- moe_gain: float32 [2048], replicated, may hold values from 0.25 to 1.75
- expert_ids: int32 [16384, 6], P(('expert', 'dp')), may hold values from 0 to 63, all different within a row; in each aligned block of 64 rows (0 to 63, 64 to 127, ...) at most 12 rows name the same one
- route_weights: float32 [16384, 6], P(('expert', 'dp')), may hold values from 0.05 to 0.4
- w_gate: bfloat16 [64, 2048, 1408], P('expert', 'dp'), may hold values from -0.125 to 0.125
- w_up: bfloat16 [64, 2048, 1408], P('expert', 'dp'), may hold values from -0.125 to 0.125
- w_down: bfloat16 [64, 1408, 2048], P('expert', 'dp'), may hold values from -0.15625 to 0.15625
- final_gain: float32 [2048], replicated, may hold values from 0.25 to 1.75
Outputs:
- layer_out: bfloat16 [16384, 2048], P(('expert', 'dp'))
The draws below stay inside these ranges and needn't reach their ends.
Inputs may be any that keep to these rules, and one draw needn't show every extreme that they name: `page_table`: the 4 pages of sequence s are distinct pages of group s // 4, which owns pages g * 16 to g * 16 + 15; every page belongs to exactly one sequence. `ctx_lens`: the first row of every sequence reads all 256 positions. `expert_ids`: each row names 6 distinct experts; among the 64 rows of one device (aligned blocks of 64 rows) no expert is named more than 12 times.
All inputs are finite; a program needn't handle non-finite values.
Results may differ from the reference program's by a relative error of at most 0.017.
Values may be sent and summed in bfloat16 or wider, within the bound.
A program may use at most 128 MiB of HBM per device.

```python
import math
import jax
import jax.numpy as jnp
import numpy as np
from jax import lax

D = 2048
HEADS = 16
HD = 128
FF = 1408
TOP = 6
R = 64
SEQ_ROWS = 64
PPS = 4
PAGE = 64
EXPERTS = 64
CTX = 256
CAP = 12
ROWS = 16384
SEQS = 256
PAGES_GRP = 16
POOL = 1024
BLOCKS = 256


def page_layout(key):
    groups = POOL // PAGES_GRP
    keys = jax.random.split(jax.random.fold_in(key, 101), groups)

    def one_group(group_key):
        return jax.random.permutation(group_key, PAGES_GRP)
    perms = jax.vmap(one_group)(keys).astype(jnp.int32)
    base = (jnp.arange(groups, dtype=jnp.int32) * PAGES_GRP)[:, None]
    return (perms + base).reshape(SEQS, PPS)


def cache_values(key):
    raw = jnp.clip(jax.random.normal(jax.random.fold_in(key, 202), (2, POOL, PAGE, D), jnp.float32), -5.0, 5.0)
    return raw


def draw_page_table(key, part):
    return page_layout(key)


def draw_kv_pool(key, part):
    return cache_values(key).astype(jnp.bfloat16)


def draw_ctx_lens(key, part):
    lens = jax.random.randint(jax.random.fold_in(key, 404), (ROWS,), 2, CTX + 1, jnp.int32)
    leading = jnp.arange(ROWS, dtype=jnp.int32) % SEQ_ROWS == 0
    return jnp.where(leading, CTX, lens).astype(jnp.int32)


def draw_queries(key, part):
    raw = jnp.clip(jax.random.normal(jax.random.fold_in(key, 303), (ROWS, D), jnp.float32), -5.0, 5.0)
    return raw.astype(jnp.bfloat16)


def levels(stream_key, shape, cuts, low, top_value):
    loudness = 1.0
    for axis_at, parts in cuts:
        steps = jax.random.uniform(jax.random.fold_in(jax.random.fold_in(stream_key, 6), axis_at), (parts,), jnp.float32, low / len(cuts), top_value / len(cuts))
        loudness = loudness * jnp.repeat(jnp.exp(steps), shape[axis_at] // parts).reshape((-1,) + (1,) * (len(shape) - 1 - axis_at))
    return loudness


def shared_out(own_key, own, number, rows, count, top, reach, lean):
    sequence = jax.random.permutation(own_key, count)
    packed, ordinary = load_shares(count, rows * top, reach, lean, True), load_shares(count, rows * top, reach, lean, False)
    places = jnp.arange(count)

    def named(tallies, rotation):
        used = int((tallies > 0).sum())
        fixed = max(1, used // 4)
        passed = fixed + (places - fixed + rotation * (used - fixed)) % max(1, count - fixed)
        return jnp.zeros((count,), jnp.int32).at[sequence[jnp.where(places < fixed, places, passed)]].set(jnp.asarray(tallies, jnp.int32))

    tallies = jnp.where(number % 4 == 0, named(packed, number // 4), named(ordinary, number - number // 4 - 1))
    mixed = jax.random.permutation(jax.random.fold_in(own, 3), count)
    giver, receiver = mixed[0:count // 2 * 2:2], mixed[1:count // 2 * 2:2]
    margin = jnp.minimum(tallies[giver] - 1, reach - tallies[receiver]) // 2
    margin = jnp.where((giver == sequence[0]) | (receiver == sequence[0]) | (tallies[receiver] == 0), 0, jnp.maximum(margin, 0))
    passed = jax.random.randint(jax.random.fold_in(own, 4), (count // 2,), 0, 1 << 20) % (margin + 1)
    tallies = tallies.at[giver].add(-passed).at[receiver].add(passed)
    members = jnp.searchsorted(jnp.cumsum(tallies), jnp.arange(rows * top), side="right").astype(jnp.int32)
    listing = members.reshape(top, rows).T
    listing = listing[jax.random.permutation(jax.random.fold_in(own, 1), rows)]
    rotation = jax.random.randint(jax.random.fold_in(own, 2), (rows, 1), 0, top)
    return jnp.take_along_axis(listing, (jnp.arange(top)[None, :] + rotation) % top, axis=1)


def load_shares(amount, total, bound, slope, full):
    loads = [(1 << 20) // math.isqrt(grade ** slope) + 1 for grade in range(1, amount + 1)]
    largest = bound if full else min(bound, max(-(-total // amount), total * loads[0] // sum(loads)))
    least = 1 if total - largest >= amount - 1 else 0
    holding, surplus = [largest] + [least] * (amount - 1), total - largest - least * (amount - 1)
    while surplus > 0:
        movable = [i for i in range(1, amount) if holding[i] < largest] or [i for i in range(1, amount) if holding[i] < bound]
        mass, left = sum([loads[i] for i in movable]), surplus
        for i in movable:
            addition = min(bound - holding[i], max(1, left * loads[i] // mass), surplus)
            holding[i] = holding[i] + addition
            surplus = surplus - addition
    return np.array(holding)


def centred(own_key, shape, width, most, pieces=(), held_as=jnp.bfloat16):
    result = jax.random.normal(own_key, shape, jnp.float32) * width
    if len(pieces) > 0:
        result = levels(own_key, shape, pieces, -0.22, 0.18) * result
    return jnp.clip(result, min=-most, max=most).astype(held_as)


def setup_inputs(seed: int = 0) -> dict:
    seeds = jax.random.split(jax.random.key(seed), 14)
    queries = draw_queries(jax.random.fold_in(seeds[13], 71), 0)
    kv_pool = draw_kv_pool(jax.random.fold_in(seeds[13], 71), 0)
    page_table = draw_page_table(jax.random.fold_in(seeds[13], 71), 0)
    ctx_lens = draw_ctx_lens(jax.random.fold_in(seeds[13], 71), 0)
    w_out = centred(seeds[4], (D, D), 0.1, 0.59765625, ((0, 4), (1, 64)))
    residual = centred(seeds[5], (ROWS, D), 0.5, 3.0, ((0, 256),))
    moe_gain = jnp.clip(1.0 + 0.15 * jax.random.normal(seeds[6], (D,), jnp.float32), 0.25, 1.75)
    expert_ids_keys = jax.random.split(jax.random.fold_in(seeds[7], 1), ROWS // R)
    expert_ids_turns = jax.random.permutation(jax.random.fold_in(seeds[7], 3), ROWS // R)
    expert_ids = jax.vmap(lambda own, number: shared_out(jax.random.fold_in(seeds[7], 2), own, number, R, EXPERTS, TOP, CAP, 2))(expert_ids_keys, expert_ids_turns).reshape((ROWS, TOP))
    route_weights = jnp.clip(0.05 + 0.35 * jax.random.uniform(seeds[8], (ROWS, TOP), jnp.float32) ** levels(seeds[8], (ROWS, TOP), ((0, 256),), -0.2, 0.2), 0.05, 0.4)
    w_gate = centred(seeds[9], (EXPERTS, D, FF), D ** -0.5, 0.125, ((0, 64), (1, 4)))
    w_up = centred(seeds[10], (EXPERTS, D, FF), D ** -0.5, 0.125, ((0, 64), (1, 4)))
    w_down = centred(seeds[11], (EXPERTS, FF, D), FF ** -0.5, 0.15625, ((0, 64), (1, 4)))
    final_gain = jnp.clip(1.0 + 0.15 * jax.random.normal(seeds[12], (D,), jnp.float32), 0.25, 1.75)
    return dict(queries=queries, kv_pool=kv_pool, page_table=page_table, ctx_lens=ctx_lens, w_out=w_out, residual=residual, moe_gain=moe_gain, expert_ids=expert_ids, route_weights=route_weights, w_gate=w_gate, w_up=w_up, w_down=w_down, final_gain=final_gain)


def normalize(values, gain):
    mean_sq = lax.optimization_barrier(jnp.mean(values * values, axis=-1, keepdims=True))
    return values * lax.rsqrt(mean_sq + 1e-06) * gain

def reference(queries, kv_pool, page_table, ctx_lens, w_out, residual, moe_gain, expert_ids, route_weights, w_gate, w_up, w_down, final_gain):
    scale = 1.0 / math.sqrt(HD)
    asked = queries.reshape(SEQS, SEQ_ROWS, HEADS, HD)
    lengths_all = ctx_lens.reshape(SEQS, SEQ_ROWS)

    def attend(inputs):
        query, pages, lengths = inputs
        keys = kv_pool[0][pages].reshape(CTX, HEADS, HD).astype(jnp.float32)
        values = kv_pool[1][pages].reshape(CTX, HEADS, HD).astype(jnp.float32)
        scores = jnp.einsum('qhd,khd->hqk', query.astype(jnp.float32), keys) * scale
        visible = (jnp.arange(CTX, dtype=jnp.int32)[None, :] < lengths[:, None])[None]
        scores = jnp.where(visible, scores, -1e+30)
        top_score = lax.optimization_barrier(jnp.max(scores, axis=-1, keepdims=True))
        expo = jnp.where(visible, jnp.exp(scores - top_score), 0.0)
        probs = (expo / lax.optimization_barrier(jnp.sum(expo, axis=-1, keepdims=True))).astype(jnp.bfloat16)
        mixed = jnp.einsum('hqk,khd->qhd', probs.astype(jnp.float32), values)
        return mixed.astype(jnp.bfloat16).reshape(SEQ_ROWS, D)
    context = lax.map(attend, (asked, page_table, lengths_all)).reshape(ROWS, D)
    projected = jnp.dot(context, w_out, preferred_element_type=jnp.float32)
    hidden_state = residual.astype(jnp.float32) + projected
    moe_input = normalize(hidden_state, moe_gain).astype(jnp.bfloat16)
    pairs = expert_ids.reshape(BLOCKS, R * TOP)
    marks = (pairs[:, :, None] == jnp.arange(EXPERTS, dtype=jnp.int32)[None, None, :]).astype(jnp.int32)
    before = lax.optimization_barrier(jnp.sum((jnp.cumsum(marks, axis=1) - 1) * marks, axis=2))
    block_ids = jnp.arange(BLOCKS, dtype=jnp.int32)[:, None]
    target = (pairs * BLOCKS + block_ids) * CAP + before
    owner = block_ids * R + (jnp.arange(R * TOP, dtype=jnp.int32) // TOP)[None, :]
    table = jnp.full((EXPERTS * BLOCKS * CAP,), ROWS, dtype=jnp.int32)
    table = table.at[target.reshape(-1)].set(owner.reshape(-1))
    padded = jnp.concatenate([moe_input, jnp.zeros((1, D), jnp.bfloat16)], axis=0)

    def run_expert(inputs):
        chosen, gate_w, up_w, down_w = inputs
        rows_in = padded[chosen]
        gate = jnp.dot(rows_in, gate_w, preferred_element_type=jnp.float32)
        up_part = jnp.dot(rows_in, up_w, preferred_element_type=jnp.float32)
        expert_mid = (jax.nn.silu(gate) * up_part).astype(jnp.bfloat16)
        return jnp.dot(expert_mid, down_w, preferred_element_type=jnp.float32).astype(jnp.bfloat16)
    outputs = lax.map(run_expert, (table.reshape(EXPERTS, BLOCKS * CAP), w_gate, w_up, w_down))
    outputs = outputs.reshape(EXPERTS * BLOCKS * CAP, D)
    answers = outputs[target.reshape(ROWS, TOP)]
    moe = lax.optimization_barrier(jnp.sum(route_weights[:, :, None] * answers.astype(jnp.float32), axis=1))
    combined = hidden_state + moe
    return normalize(combined, final_gain).astype(jnp.bfloat16)
```

```python
import functools
import math

import jax
import jax.numpy as jnp
from jax import lax
from jax.experimental import pallas as pl
from jax.experimental.pallas import tpu as pltpu
from jax.sharding import PartitionSpec as P

HD = 128
TOP = 6
CTX = 256
CAP = 12
NP = 8
CHUNKS = 4
MESH = pl.DeviceIdType.MESH
F32 = jnp.float32
BF16 = jnp.bfloat16


def normalize(values, gain):
    mean_sq = jnp.mean(values * values, axis=-1, keepdims=True)
    return values * lax.rsqrt(mean_sq + 1e-06) * gain


def iota(shape, axis):
    return lax.broadcasted_iota(jnp.int32, shape, axis)


def dot(a, b):
    return jnp.dot(a, b, preferred_element_type=F32)


def moe_kernel(
    sizes,
    x_ref,
    hid_ref,
    ids_ref,
    rw_ref,
    wg_ref,
    wu_ref,
    wd_ref,
    gain_ref,
    out_ref,
    wgf,
    wuf,
    wdf,
    rows,
    route_out,
    route,
    snd,
    xin,
    mid,
    yout,
    ans,
    wcomb,
    psnd,
    prcv,
    comb,
    loc_sem,
    gu_s,
    gu_r,
    wd_s,
    wd_r,
    za_s,
    za_r,
    ya_s,
    ya_r,
    ry_s,
    ry_r,
    rz_s,
    rz_r,
):
    nd, nz, order = sizes
    pos = {off: i for i, off in enumerate(order)}
    groups = 2
    per = nz // groups
    d = lax.axis_index("dp")
    e = lax.axis_index("expert")
    z = e // NP
    p = lax.rem(e, NP)
    n_rows, width = x_ref.shape
    kd = wg_ref.shape[0]
    ff = wg_ref.shape[1]
    kf = wd_ref.shape[0]
    cw = width // CHUNKS
    seg = per * CAP
    gsz = NP * seg
    right = lax.rem(d + 1, nd)
    left = lax.rem(d + nd - 1, nd)
    sends = []

    def plane(j):
        return (d, z * NP + lax.rem(p + j, NP))

    def line(off):
        return (d, lax.rem(z + off, nz) * NP + p)

    def remote(src, dst, s, r, to):
        c = pltpu.make_async_remote_copy(
            src_ref=src, dst_ref=dst, send_sem=s, recv_sem=r, device_id=to, device_id_type=MESH
        )
        c.start()
        sends.append(c)
        return c

    barrier = pltpu.get_barrier_semaphore()
    peers = [(right, e), (left, e)] + [line(o) for o in range(1, nz)] + [plane(j) for j in range(1, NP)]
    for peer in peers:
        pl.semaphore_signal(barrier, inc=1, device_id=peer, device_id_type=MESH)
    pl.semaphore_wait(barrier, len(peers))

    rows[pl.ds(0, n_rows), :] = x_ref[...]
    lanes = ids_ref.shape[1]
    experts = nz * NP
    named = jnp.zeros((experts, lanes), F32)
    share = jnp.zeros((experts, lanes), F32)
    for k in range(TOP):
        hit = ids_ref[k : k + 1, :] == iota((experts, lanes), 0)
        named = named + jnp.where(hit, 1.0, 0.0)
        share = share + jnp.where(hit, rw_ref[k : k + 1, :], 0.0)
    upper = jnp.where(iota((lanes, lanes), 0) < iota((lanes, lanes), 1), 1.0, 0.0).astype(BF16)
    rank = dot(named.astype(BF16), upper)
    rank = jnp.where(named > 0.5, rank, -1.0)
    for i in range(nz):
        route_out[i, 0:NP, :] = rank[i * NP : (i + 1) * NP, :]
        route_out[i, NP : 2 * NP, :] = share[i * NP : (i + 1) * NP, :]
    own_route = pltpu.make_async_copy(route_out.at[z], route.at[0], loc_sem.at[3])
    own_route.start()
    za = {}
    for off in order[1:]:
        slot = pos[nz - off]
        zt = lax.rem(z + off, nz)
        a = remote(route_out.at[zt], route.at[slot], za_s.at[0, off], za_r.at[0, slot], line(off))
        b = remote(
            x_ref, rows.at[pl.ds(slot * n_rows, n_rows), :], za_s.at[1, off], za_r.at[1, slot], line(off)
        )
        za[slot] = (a, b)

    gu = [(wg_ref, wgf), (wu_ref, wuf)]
    half = kd // 2
    local = []
    for m, (src, dst) in enumerate(gu):
        c = pltpu.make_async_copy(src, dst.at[pl.ds(d * kd, kd), :], loc_sem.at[m])
        c.start()
        local.append(c)
    c = pltpu.make_async_copy(wd_ref, wdf.at[pl.ds(d * kf, kf), :], loc_sem.at[2])
    c.start()
    local.append(c)
    gu_c = {}
    for m, (src, dst) in enumerate(gu):
        for side, to in ((0, right), (1, left)):
            for h in (side, 1 - side):
                gu_c[m, side, h] = remote(
                    src.at[pl.ds(h * half, half), :],
                    dst.at[pl.ds(d * kd + h * half, half), :],
                    gu_s.at[m, side, h],
                    gu_r.at[m, side, h],
                    (to, e),
                )

    slot_i = iota((gsz, per * n_rows), 0)
    expand = jnp.where(iota((gsz, NP), 0) // seg == iota((gsz, NP), 1), 1.0, 0.0).astype(BF16)
    want = lax.rem(slot_i, CAP).astype(F32)
    block_ok = lax.rem(slot_i, seg) // CAP == iota((gsz, per * n_rows), 1) // n_rows
    ya = {}

    def dispatch(g):
        for i in range(g * per, (g + 1) * per):
            if i == 0:
                own_route.wait()
            else:
                za[i][0].wait_recv()
                za[i][1].wait_recv()
        ranks = jnp.concatenate(
            [route[i, 0:NP, 0:n_rows] for i in range(g * per, (g + 1) * per)], axis=1
        )
        shares = jnp.concatenate(
            [route[i, NP : 2 * NP, 0:n_rows] for i in range(g * per, (g + 1) * per)], axis=1
        )
        pick = jnp.logical_and(dot(expand, ranks.astype(BF16)) == want, block_ok)
        pick_b = jnp.where(pick, 1.0, 0.0).astype(BF16)
        base = g * per * n_rows

        def tile(i, carry):
            cols = pl.ds(pl.multiple_of(i * 512, 512), 512)
            snd[g, :, cols] = dot(pick_b, rows[pl.ds(base, per * n_rows), cols]).astype(BF16)
            return carry

        lax.fori_loop(0, width // 512, tile, 0)
        for j in range(1, NP):
            t = lax.rem(p + j, NP)
            ya[g, j] = remote(
                snd.at[g, pl.ds(t * seg, seg), :],
                xin.at[g, pl.ds(p * seg, seg), :],
                ya_s.at[g, j],
                ya_r.at[g, j],
                plane(j),
            )
        mine = pltpu.make_async_copy(
            snd.at[g, pl.ds(p * seg, seg), :], xin.at[g, pl.ds(p * seg, seg), :], ya_s.at[g, 0]
        )
        mine.start()
        ya[g, 0] = mine
        hi = shares.astype(BF16)
        lo = (shares - hi.astype(F32)).astype(BF16)
        for part, val in ((0, hi), (1, lo)):
            full = jnp.where(pick, dot(expand, val), 0.0)
            wcomb[g, part] = jnp.transpose(full).astype(BF16)

    for g in range(groups):
        dispatch(g)

    gu_f = {}
    for m, (_, dst) in enumerate(gu):
        for side, frm, to in ((0, left, right), (1, right, left)):
            gu_c[m, side, side].wait_recv()
            at = pl.ds(frm * kd + side * half, half)
            gu_f[m, side] = remote(
                dst.at[at, :], dst.at[at, :], gu_s.at[m, side, 2], gu_r.at[m, side, 2], (to, e)
            )
    hf = kf // 2
    wd_c = {}
    for n in range(CHUNKS):
        cols = pl.ds(n * cw, cw)
        for side, to in ((0, right), (1, left)):
            for h in (side, 1 - side):
                wd_c[n, side, h] = remote(
                    wd_ref.at[pl.ds(h * hf, hf), cols],
                    wdf.at[pl.ds(d * kf + h * hf, hf), cols],
                    wd_s.at[n, side, h],
                    wd_r.at[n, side, h],
                    (to, e),
                )
    for m in range(2):
        local[m].wait()
        for side in range(2):
            gu_c[m, side, 1 - side].wait_recv()
            gu_f[m, side].wait_recv()
    wd_f = {}
    for n in range(CHUNKS):
        cols = pl.ds(n * cw, cw)
        for side, frm, to in ((0, left, right), (1, right, left)):
            wd_c[n, side, side].wait_recv()
            at = pl.ds(frm * kf + side * hf, hf)
            wd_f[n, side] = remote(
                wdf.at[at, cols], wdf.at[at, cols], wd_s.at[n, side, 2], wd_r.at[n, side, 2], (to, e)
            )

    def up_tile(g, cols):
        xs = xin[g]
        gate = dot(xs, wgf[:, cols])
        up = dot(xs, wuf[:, cols])
        mid[g, :, cols] = (gate / (1.0 + jnp.exp(-gate)) * up).astype(BF16)

    full_tiles = ff // 256
    for g in range(groups):
        for j in range(1, NP):
            ya[g, j].wait_recv()
        ya[g, 0].wait()

        def step(i, carry, g=g):
            up_tile(g, pl.ds(pl.multiple_of(i * 256, 256), 256))
            return carry

        lax.fori_loop(0, full_tiles, step, 0)
        if ff % 256:
            up_tile(g, pl.ds(full_tiles * 256, ff % 256))

    ry = {}
    rz = {}

    def down(n, g):
        def tile(i, carry):
            c0 = pl.multiple_of(i * 256, 256)
            val = dot(mid[g], wdf[:, pl.ds(pl.multiple_of(n * cw + i * 256, 256), 256)])
            yout[n, g, :, pl.ds(c0, 256)] = val.astype(BF16)
            return carry

        lax.fori_loop(0, cw // 256, tile, 0)
        for j in range(1, NP):
            t = lax.rem(p + j, NP)
            ry[n, g, j] = remote(
                yout.at[n, g, pl.ds(t * seg, seg), :],
                ans.at[n, g, pl.ds(p * seg, seg), :],
                ry_s.at[n, g, j],
                ry_r.at[n, g, j],
                plane(j),
            )
        mine = pltpu.make_async_copy(
            yout.at[n, g, pl.ds(p * seg, seg), :],
            ans.at[n, g, pl.ds(p * seg, seg), :],
            ry_s.at[n, g, 0],
        )
        mine.start()
        ry[n, g, 0] = mine

    def combine(n, g):
        for j in range(1, NP):
            ry[n, g, j].wait_recv()
        ry[n, g, 0].wait()
        part = dot(wcomb[g, 0], ans[n, g]) + dot(wcomb[g, 1], ans[n, g])
        psnd[n, pl.ds(g * per * n_rows, per * n_rows), :] = part.astype(BF16)
        for i in range(g * per, (g + 1) * per):
            off = order[i]
            if off == 0:
                continue
            slot = pos[nz - off]
            rz[n, slot] = remote(
                psnd.at[n, pl.ds(i * n_rows, n_rows), :],
                prcv.at[n, pl.ds(slot * n_rows, n_rows), :],
                rz_s.at[n, i],
                rz_r.at[n, slot],
                line(off),
            )

    def gather_home(n):
        total = psnd[n, 0:n_rows, :].astype(F32)
        for slot in range(1, nz):
            rz[n, slot].wait_recv()
            total = total + prcv[n, slot * n_rows : (slot + 1) * n_rows, :].astype(F32)
        cols = slice(n * cw, (n + 1) * cw)
        comb[:, cols] = hid_ref[:, cols] + total

    local[2].wait()
    for n in range(CHUNKS):
        for side in range(2):
            wd_c[n, side, 1 - side].wait_recv()
            wd_f[n, side].wait_recv()
        for g in range(groups):
            down(n, g)
        if n >= 1:
            for g in range(groups):
                combine(n - 1, g)
        if n >= 2:
            gather_home(n - 2)
    for g in range(groups):
        combine(CHUNKS - 1, g)
    gather_home(CHUNKS - 2)
    gather_home(CHUNKS - 1)
    out_ref[...] = normalize(comb[...], gain_ref[...]).astype(BF16)
    for c in sends:
        c.wait_send()


def moe(x, hidden, ids, shares, w_gate, w_up, w_down, gain):
    nd = lax.axis_size("dp")
    experts = lax.axis_size("expert")
    nz = experts // NP
    order = [0]
    for k in range(1, nz // 2 + 1):
        order.append(k)
        if nz - k != k:
            order.append(nz - k)
    n_rows, width = x.shape
    kd, ff = w_gate.shape
    kf = w_down.shape[0]
    cw = width // CHUNKS
    per = nz // 2
    seg = per * CAP
    gsz = NP * seg
    vmem = pl.BlockSpec(memory_space=pltpu.VMEM)
    hbm = pl.BlockSpec(memory_space=pl.ANY)
    dma = pltpu.SemaphoreType.DMA
    return pl.pallas_call(
        functools.partial(moe_kernel, (nd, nz, order)),
        out_shape=jax.ShapeDtypeStruct((n_rows, width), BF16),
        in_specs=[vmem, vmem, vmem, vmem, hbm, hbm, hbm, vmem],
        out_specs=vmem,
        scratch_shapes=[
            pltpu.VMEM((nd * kd, ff), BF16),
            pltpu.VMEM((nd * kd, ff), BF16),
            pltpu.VMEM((nd * kf, width), BF16),
            pltpu.VMEM((nz * n_rows, width), BF16),
            pltpu.VMEM((nz, 2 * NP, 128), F32),
            pltpu.VMEM((nz, 2 * NP, 128), F32),
            pltpu.VMEM((2, gsz, width), BF16),
            pltpu.VMEM((2, gsz, width), BF16),
            pltpu.VMEM((2, gsz, ff), BF16),
            pltpu.VMEM((CHUNKS, 2, gsz, cw), BF16),
            pltpu.VMEM((CHUNKS, 2, gsz, cw), BF16),
            pltpu.VMEM((2, 2, per * n_rows, gsz), BF16),
            pltpu.VMEM((CHUNKS, nz * n_rows, cw), BF16),
            pltpu.VMEM((CHUNKS, nz * n_rows, cw), BF16),
            pltpu.VMEM((n_rows, width), F32),
            dma((4,)),
            dma((2, 2, 3)),
            dma((2, 2, 3)),
            dma((CHUNKS, 2, 3)),
            dma((CHUNKS, 2, 3)),
            dma((2, nz)),
            dma((2, nz)),
            dma((2, NP)),
            dma((2, NP)),
            dma((CHUNKS, 2, NP)),
            dma((CHUNKS, 2, NP)),
            dma((CHUNKS, nz)),
            dma((CHUNKS, nz)),
        ],
        compiler_params=pltpu.CompilerParams(
            collective_id=0, has_side_effects=True, vmem_limit_bytes=60 << 20
        ),
    )(x, hidden, ids, shares, w_gate, w_up, w_down, gain)


def shards(
    queries,
    kv_pool,
    page_table,
    ctx_lens,
    w_out,
    residual,
    moe_gain,
    expert_ids,
    route_weights,
    w_gate,
    w_up,
    w_down,
    final_gain,
):
    scale = 1.0 / math.sqrt(HD)
    group_rows = queries.shape[0]
    local_feats = queries.shape[1]
    local_heads = local_feats // HD
    seq_count = page_table.shape[0]
    seq_rows = group_rows // seq_count
    pool_here = kv_pool.shape[1]
    local_pages = page_table - lax.axis_index("expert") * pool_here
    keys = kv_pool[0][local_pages].reshape(seq_count, CTX, local_heads, HD)
    values = kv_pool[1][local_pages].reshape(seq_count, CTX, local_heads, HD)
    asked = queries.reshape(seq_count, seq_rows, local_heads, HD)
    scores = jnp.einsum("sqhd,skhd->shqk", asked, keys, preferred_element_type=F32) * scale
    lengths = ctx_lens.reshape(seq_count, seq_rows)
    visible = (jnp.arange(CTX, dtype=jnp.int32)[None, None, :] < lengths[:, :, None])[:, None]
    scores = jnp.where(visible, scores, -1e30)
    top_score = jnp.max(scores, axis=-1, keepdims=True)
    expo = jnp.where(visible, jnp.exp(scores - top_score), 0.0)
    probs = (expo / jnp.sum(expo, axis=-1, keepdims=True)).astype(BF16)
    mixed = jnp.einsum("shqk,skhd->sqhd", probs, values, preferred_element_type=F32)
    context = mixed.astype(BF16).reshape(group_rows, local_feats)
    columns = lax.all_gather(w_out, "expert", axis=1, tiled=True)
    projected = lax.psum_scatter(
        jnp.dot(context, columns, preferred_element_type=F32).astype(BF16),
        "dp",
        scatter_dimension=0,
        tiled=True,
    ).astype(F32)
    hidden_state = residual.astype(F32) + projected
    moe_input = normalize(hidden_state, moe_gain).astype(BF16)
    rows_here = moe_input.shape[0]
    ids = jnp.full((8, 128), -1, jnp.int32).at[:TOP, :rows_here].set(expert_ids.T)
    shares = jnp.zeros((8, 128), F32).at[:TOP, :rows_here].set(route_weights.T)
    return moe(
        moe_input, hidden_state, ids, shares, w_gate[0], w_up[0], w_down[0], final_gain[None, :]
    )


def solution(mesh):
    return jax.shard_map(
        shards,
        mesh=mesh,
        in_specs=(
            P("expert", "dp"),
            P(None, "expert", None, "dp"),
            P("expert", None),
            P("expert"),
            P("dp", "expert"),
            P(("expert", "dp"), None),
            P(),
            P(("expert", "dp"), None),
            P(("expert", "dp"), None),
            P("expert", "dp", None),
            P("expert", "dp", None),
            P("expert", "dp", None),
            P(),
        ),
        out_specs=P(("expert", "dp"), None),
        check_vma=False,
    )
```

```python
import functools
import math

import jax
import jax.numpy as jnp
from jax import lax
from jax.experimental import pallas as pl
from jax.experimental.pallas import tpu as pltpu
from jax.sharding import PartitionSpec as P

HD = 128
TOP = 6
CAP = 12
NP = 8
CHUNKS = 4
MESH = pl.DeviceIdType.MESH
F32 = jnp.float32
BF16 = jnp.bfloat16


def normalize(values, gain):
    mean_sq = jnp.mean(values * values, axis=-1, keepdims=True)
    return values * lax.rsqrt(mean_sq + 1e-06) * gain


def iota(shape, axis):
    return lax.broadcasted_iota(jnp.int32, shape, axis)


def dot(a, b):
    return jnp.dot(a, b, preferred_element_type=F32)


def moe_kernel(
    sizes,
    table_ref,
    q_ref,
    kv_ref,
    lens_ref,
    wot_ref,
    res_ref,
    mgain_ref,
    ids_ref,
    rw_ref,
    wg_ref,
    wu_ref,
    wd_ref,
    gain_ref,
    out_ref,
    kvs,
    keys,
    vals,
    ctx,
    wo,
    prs,
    prr,
    hid,
    wgf,
    wuf,
    wdf,
    rows,
    route_out,
    route,
    snd,
    xin,
    mid,
    yout,
    ans,
    wcomb,
    psnd,
    prcv,
    comb,
    loc_sem,
    w1_s,
    w1_r,
    w2_s,
    w2_r,
    w3_s,
    w3_r,
    pr_s,
    pr_r,
    gu_s,
    gu_r,
    wd_s,
    wd_r,
    za_s,
    za_r,
    ya_s,
    ya_r,
    ry_s,
    ry_r,
    rz_s,
    rz_r,
):
    nd, nz, order = sizes
    pos = {off: i for i, off in enumerate(order)}
    groups = 2
    per = nz // groups
    d = lax.axis_index("dp")
    e = lax.axis_index("expert")
    z = e // NP
    p = lax.rem(e, NP)
    n_rows, width = res_ref.shape
    kd = wg_ref.shape[0]
    ff = wg_ref.shape[1]
    kf = wd_ref.shape[0]
    cw = width // CHUNKS
    seg = per * CAP
    gsz = NP * seg
    right = lax.rem(d + 1, nd)
    left = lax.rem(d + nd - 1, nd)
    sends = []

    def plane(j):
        return (d, z * NP + lax.rem(p + j, NP))

    def line(off):
        return (d, lax.rem(z + off, nz) * NP + p)

    def across(k):
        return (lax.rem(d + k, nd), e)

    def remote(src, dst, s, r, to):
        c = pltpu.make_async_remote_copy(
            src_ref=src, dst_ref=dst, send_sem=s, recv_sem=r, device_id=to, device_id_type=MESH
        )
        c.start()
        sends.append(c)
        return c

    kv_c = pltpu.make_async_copy(kv_ref, kvs, loc_sem.at[4])
    kv_c.start()
    barrier = pltpu.get_barrier_semaphore()
    peers = [across(k) for k in range(1, nd)]
    peers += [line(o) for o in range(1, nz)] + [plane(j) for j in range(1, NP)]
    for peer in peers:
        pl.semaphore_signal(barrier, inc=1, device_id=peer, device_id_type=MESH)
    wo[z, p] = wot_ref[...]
    pl.semaphore_wait(barrier, len(peers))

    w1 = {}
    for off in order[1:]:
        w1[off] = remote(wot_ref, wo.at[z, p], w1_s.at[off], w1_r.at[off], line(off))

    gu = [(wg_ref, wgf), (wu_ref, wuf)]
    half = kd // 2
    gu_c = {}

    def ring_start(m):
        src, dst = gu[m]
        for side, to in ((0, right), (1, left)):
            for h in (side, 1 - side):
                gu_c[m, side, h] = remote(
                    src.at[pl.ds(h * half, half), :],
                    dst.at[pl.ds(d * kd + h * half, half), :],
                    gu_s.at[m, side, h],
                    gu_r.at[m, side, h],
                    (to, e),
                )

    ring_start(0)

    experts = nz * NP
    lanes = 128
    named = jnp.zeros((n_rows, lanes), F32)
    share = jnp.zeros((n_rows, lanes), F32)
    for k in range(TOP):
        hit = ids_ref[:, k : k + 1] == iota((n_rows, lanes), 1)
        named = named + jnp.where(hit, 1.0, 0.0)
        share = share + jnp.where(hit, rw_ref[:, k : k + 1], 0.0)
    named = jnp.transpose(named)
    share = jnp.transpose(share)
    upper = jnp.where(iota((n_rows, n_rows), 0) < iota((n_rows, n_rows), 1), 1.0, 0.0).astype(BF16)
    rank = dot(named.astype(BF16), upper)
    rank = jnp.where(named > 0.5, rank, -1.0)
    for i in range(nz):
        route_out[i, 0:NP, :] = rank[i * NP : (i + 1) * NP, :]
        route_out[i, NP : 2 * NP, :] = share[i * NP : (i + 1) * NP, :]
    own_route = pltpu.make_async_copy(route_out.at[z], route.at[0], loc_sem.at[3])
    own_route.start()
    zr = {}
    for off in order[1:]:
        slot = pos[nz - off]
        zt = lax.rem(z + off, nz)
        zr[slot] = remote(
            route_out.at[zt], route.at[slot], za_s.at[0, off], za_r.at[0, slot], line(off)
        )

    for off in order[1:]:
        w1[off].wait_recv()
    sib = p + 1 - 2 * lax.rem(p, 2)
    sib_to = (d, z * NP + sib)
    w2 = {}
    w3 = {}
    for k in range(1, NP // 2):
        w2[k] = remote(wo.at[:, p], wo.at[:, p], w2_s.at[k], w2_r.at[k], plane(2 * k))
    w3[0] = remote(wo.at[:, p], wo.at[:, p], w3_s.at[0], w3_r.at[0], sib_to)

    seqs = table_ref.shape[0]
    pages = table_ref.shape[1]
    pool = kv_ref.shape[1]
    page = kv_ref.shape[2]
    span = pages * page
    q_rows = q_ref.shape[0] // seqs
    scale = 1.0 / math.sqrt(HD)
    kv_c.wait()

    def attend(s, carry):
        for i in range(pages):
            at = lax.rem(table_ref[s, i], pool)
            keys[i * page : (i + 1) * page, :] = kvs[0, at]
            vals[i * page : (i + 1) * page, :] = kvs[1, at]
        here = pl.ds(pl.multiple_of(s * q_rows, q_rows), q_rows)
        seen = iota((q_rows, span), 1) < lens_ref[here, :]
        for h in range(q_ref.shape[1] // HD):
            cols = slice(h * HD, (h + 1) * HD)
            sc = lax.dot_general(
                q_ref[here, cols], keys[:, cols], (((1,), (1,)), ((), ())), preferred_element_type=F32
            )
            sc = jnp.where(seen, sc * scale, -1e30)
            ex = jnp.where(seen, jnp.exp(sc - jnp.max(sc, axis=-1, keepdims=True)), 0.0)
            pr = (ex / jnp.sum(ex, axis=-1, keepdims=True)).astype(BF16)
            ctx[here, cols] = dot(pr, vals[:, cols]).astype(BF16)
        return carry

    lax.fori_loop(0, seqs, attend, 0)

    for k in range(1, NP // 2):
        w2[k].wait_recv()
        got = lax.rem(p + NP - 2 * k, NP)
        w3[k] = remote(wo.at[:, got], wo.at[:, got], w3_s.at[k], w3_r.at[k], sib_to)
    for k in range(NP // 2):
        w3[k].wait_recv()

    wn = NP * wot_ref.shape[0]

    def project(i, carry):
        w = wo[i].reshape(wn, wot_ref.shape[1])
        val = lax.dot_general(
            ctx[...], w, (((1,), (1,)), ((), ())), preferred_element_type=F32
        ).astype(BF16)
        cols = pl.ds(pl.multiple_of(i * wn, wn), wn)
        for j in range(nd):
            prs[j, :, cols] = val[j * n_rows : (j + 1) * n_rows, :]
        return carry

    lax.fori_loop(0, nz, project, 0)
    pr = {}
    for k in (2, 1, 3):
        pr[k] = remote(
            prs.at[lax.rem(d + k, nd)], prr.at[k], pr_s.at[k], pr_r.at[k], across(k)
        )
    ring_start(1)
    local = []
    for m, (src, dst) in enumerate(gu):
        c = pltpu.make_async_copy(src, dst.at[pl.ds(d * kd, kd), :], loc_sem.at[m])
        c.start()
        local.append(c)
    c = pltpu.make_async_copy(wd_ref, wdf.at[pl.ds(d * kf, kf), :], loc_sem.at[2])
    c.start()
    local.append(c)
    state = res_ref[...].astype(F32) + prs[d].astype(F32)
    for k in (1, 3, 2):
        pr[k].wait_recv()
        state = state + prr[k].astype(F32)
    hid[...] = state
    rows[pl.ds(0, n_rows), :] = normalize(state, mgain_ref[...]).astype(BF16)

    za = {}
    for off in order[1:]:
        slot = pos[nz - off]
        za[slot] = remote(
            rows.at[pl.ds(0, n_rows), :],
            rows.at[pl.ds(slot * n_rows, n_rows), :],
            za_s.at[1, off],
            za_r.at[1, slot],
            line(off),
        )

    slot_i = iota((gsz, per * n_rows), 0)
    expand = jnp.where(iota((gsz, NP), 0) // seg == iota((gsz, NP), 1), 1.0, 0.0).astype(BF16)
    want = lax.rem(slot_i, CAP).astype(F32)
    block_ok = lax.rem(slot_i, seg) // CAP == iota((gsz, per * n_rows), 1) // n_rows
    ya = {}

    def dispatch(g):
        for i in range(g * per, (g + 1) * per):
            if i == 0:
                own_route.wait()
            else:
                zr[i].wait_recv()
                za[i].wait_recv()
        ranks = jnp.concatenate(
            [route[i, 0:NP, 0:n_rows] for i in range(g * per, (g + 1) * per)], axis=1
        )
        shares = jnp.concatenate(
            [route[i, NP : 2 * NP, 0:n_rows] for i in range(g * per, (g + 1) * per)], axis=1
        )
        pick = jnp.logical_and(dot(expand, ranks.astype(BF16)) == want, block_ok)
        pick_b = jnp.where(pick, 1.0, 0.0).astype(BF16)
        base = g * per * n_rows

        def tile(i, carry):
            cols = pl.ds(pl.multiple_of(i * 512, 512), 512)
            snd[g, :, cols] = dot(pick_b, rows[pl.ds(base, per * n_rows), cols]).astype(BF16)
            return carry

        lax.fori_loop(0, width // 512, tile, 0)
        for j in range(1, NP):
            t = lax.rem(p + j, NP)
            ya[g, j] = remote(
                snd.at[g, pl.ds(t * seg, seg), :],
                xin.at[g, pl.ds(p * seg, seg), :],
                ya_s.at[g, j],
                ya_r.at[g, j],
                plane(j),
            )
        mine = pltpu.make_async_copy(
            snd.at[g, pl.ds(p * seg, seg), :], xin.at[g, pl.ds(p * seg, seg), :], ya_s.at[g, 0]
        )
        mine.start()
        ya[g, 0] = mine
        hi = shares.astype(BF16)
        lo = (shares - hi.astype(F32)).astype(BF16)
        for part, val in ((0, hi), (1, lo)):
            full = jnp.where(pick, dot(expand, val), 0.0)
            wcomb[g, part] = jnp.transpose(full).astype(BF16)

    for g in range(groups):
        dispatch(g)

    gu_f = {}
    for m, (_, dst) in enumerate(gu):
        for side, frm, to in ((0, left, right), (1, right, left)):
            gu_c[m, side, side].wait_recv()
            at = pl.ds(frm * kd + side * half, half)
            gu_f[m, side] = remote(
                dst.at[at, :], dst.at[at, :], gu_s.at[m, side, 2], gu_r.at[m, side, 2], (to, e)
            )
    hf = kf // 2
    wd_c = {}
    for n in range(CHUNKS):
        cols = pl.ds(n * cw, cw)
        for side, to in ((0, right), (1, left)):
            for h in (side, 1 - side):
                wd_c[n, side, h] = remote(
                    wd_ref.at[pl.ds(h * hf, hf), cols],
                    wdf.at[pl.ds(d * kf + h * hf, hf), cols],
                    wd_s.at[n, side, h],
                    wd_r.at[n, side, h],
                    (to, e),
                )
    for m in range(2):
        local[m].wait()
        for side in range(2):
            gu_c[m, side, 1 - side].wait_recv()
            gu_f[m, side].wait_recv()
    wd_f = {}
    for n in range(CHUNKS):
        cols = pl.ds(n * cw, cw)
        for side, frm, to in ((0, left, right), (1, right, left)):
            wd_c[n, side, side].wait_recv()
            at = pl.ds(frm * kf + side * hf, hf)
            wd_f[n, side] = remote(
                wdf.at[at, cols], wdf.at[at, cols], wd_s.at[n, side, 2], wd_r.at[n, side, 2], (to, e)
            )

    def up_tile(g, cols):
        xs = xin[g]
        gate = dot(xs, wgf[:, cols])
        up = dot(xs, wuf[:, cols])
        mid[g, :, cols] = (gate / (1.0 + jnp.exp(-gate)) * up).astype(BF16)

    full_tiles = ff // 256
    for g in range(groups):
        for j in range(1, NP):
            ya[g, j].wait_recv()
        ya[g, 0].wait()

        def step(i, carry, g=g):
            up_tile(g, pl.ds(pl.multiple_of(i * 256, 256), 256))
            return carry

        lax.fori_loop(0, full_tiles, step, 0)
        if ff % 256:
            up_tile(g, pl.ds(full_tiles * 256, ff % 256))

    ry = {}
    rz = {}

    def down(n, g):
        def tile(i, carry):
            c0 = pl.multiple_of(i * 256, 256)
            val = dot(mid[g], wdf[:, pl.ds(pl.multiple_of(n * cw + i * 256, 256), 256)])
            yout[n, g, :, pl.ds(c0, 256)] = val.astype(BF16)
            return carry

        lax.fori_loop(0, cw // 256, tile, 0)
        for j in range(1, NP):
            t = lax.rem(p + j, NP)
            ry[n, g, j] = remote(
                yout.at[n, g, pl.ds(t * seg, seg), :],
                ans.at[n, g, pl.ds(p * seg, seg), :],
                ry_s.at[n, g, j],
                ry_r.at[n, g, j],
                plane(j),
            )
        mine = pltpu.make_async_copy(
            yout.at[n, g, pl.ds(p * seg, seg), :],
            ans.at[n, g, pl.ds(p * seg, seg), :],
            ry_s.at[n, g, 0],
        )
        mine.start()
        ry[n, g, 0] = mine

    def combine(n, g):
        for j in range(1, NP):
            ry[n, g, j].wait_recv()
        ry[n, g, 0].wait()
        part = dot(wcomb[g, 0], ans[n, g]) + dot(wcomb[g, 1], ans[n, g])
        psnd[n, pl.ds(g * per * n_rows, per * n_rows), :] = part.astype(BF16)
        for i in range(g * per, (g + 1) * per):
            off = order[i]
            if off == 0:
                continue
            slot = pos[nz - off]
            rz[n, slot] = remote(
                psnd.at[n, pl.ds(i * n_rows, n_rows), :],
                prcv.at[n, pl.ds(slot * n_rows, n_rows), :],
                rz_s.at[n, i],
                rz_r.at[n, slot],
                line(off),
            )

    def gather_home(n):
        total = psnd[n, 0:n_rows, :].astype(F32)
        for slot in range(1, nz):
            rz[n, slot].wait_recv()
            total = total + prcv[n, slot * n_rows : (slot + 1) * n_rows, :].astype(F32)
        cols = slice(n * cw, (n + 1) * cw)
        comb[:, cols] = hid[:, cols] + total

    local[2].wait()
    for n in range(CHUNKS):
        for side in range(2):
            wd_c[n, side, 1 - side].wait_recv()
            wd_f[n, side].wait_recv()
        for g in range(groups):
            down(n, g)
        if n >= 1:
            for g in range(groups):
                combine(n - 1, g)
        if n >= 2:
            gather_home(n - 2)
    for g in range(groups):
        combine(CHUNKS - 1, g)
    gather_home(CHUNKS - 2)
    gather_home(CHUNKS - 1)
    out_ref[...] = normalize(comb[...], gain_ref[...]).astype(BF16)
    for c in sends:
        c.wait_send()


def shards(
    queries,
    kv_pool,
    page_table,
    ctx_lens,
    w_out,
    residual,
    moe_gain,
    expert_ids,
    route_weights,
    w_gate,
    w_up,
    w_down,
    final_gain,
):
    nd = lax.axis_size("dp")
    experts = lax.axis_size("expert")
    nz = experts // NP
    order = [0]
    for k in range(1, nz // 2 + 1):
        order.append(k)
        if nz - k != k:
            order.append(nz - k)
    n_rows, width = residual.shape
    group_rows, feats = queries.shape
    _, pool, page, _ = kv_pool.shape
    span = page_table.shape[1] * page
    wc = w_out.shape[1]
    kd, ff = w_gate.shape[1:]
    kf = w_down.shape[1]
    cw = width // CHUNKS
    per = nz // 2
    seg = per * CAP
    gsz = NP * seg
    vmem = pl.BlockSpec(memory_space=pltpu.VMEM)
    smem = pl.BlockSpec(memory_space=pltpu.SMEM)
    hbm = pl.BlockSpec(memory_space=pl.ANY)
    dma = pltpu.SemaphoreType.DMA
    return pl.pallas_call(
        functools.partial(moe_kernel, (nd, nz, order)),
        out_shape=jax.ShapeDtypeStruct((n_rows, width), BF16),
        in_specs=[smem, vmem, hbm, vmem, vmem, vmem, vmem, vmem, vmem, hbm, hbm, hbm, vmem],
        out_specs=vmem,
        scratch_shapes=[
            pltpu.VMEM((2, pool, page, feats), BF16),
            pltpu.VMEM((span, feats), BF16),
            pltpu.VMEM((span, feats), BF16),
            pltpu.VMEM((group_rows, feats), BF16),
            pltpu.VMEM((nz, NP, wc, feats), BF16),
            pltpu.VMEM((nd, n_rows, width), BF16),
            pltpu.VMEM((nd, n_rows, width), BF16),
            pltpu.VMEM((n_rows, width), F32),
            pltpu.VMEM((nd * kd, ff), BF16),
            pltpu.VMEM((nd * kd, ff), BF16),
            pltpu.VMEM((nd * kf, width), BF16),
            pltpu.VMEM((nz * n_rows, width), BF16),
            pltpu.VMEM((nz, 2 * NP, n_rows), F32),
            pltpu.VMEM((nz, 2 * NP, n_rows), F32),
            pltpu.VMEM((2, gsz, width), BF16),
            pltpu.VMEM((2, gsz, width), BF16),
            pltpu.VMEM((2, gsz, ff), BF16),
            pltpu.VMEM((CHUNKS, 2, gsz, cw), BF16),
            pltpu.VMEM((CHUNKS, 2, gsz, cw), BF16),
            pltpu.VMEM((2, 2, per * n_rows, gsz), BF16),
            pltpu.VMEM((CHUNKS, nz * n_rows, cw), BF16),
            pltpu.VMEM((CHUNKS, nz * n_rows, cw), BF16),
            pltpu.VMEM((n_rows, width), F32),
            dma((5,)),
            dma((nz,)),
            dma((nz,)),
            dma((NP // 2,)),
            dma((NP // 2,)),
            dma((NP // 2,)),
            dma((NP // 2,)),
            dma((nd,)),
            dma((nd,)),
            dma((2, 2, 3)),
            dma((2, 2, 3)),
            dma((CHUNKS, 2, 3)),
            dma((CHUNKS, 2, 3)),
            dma((2, nz)),
            dma((2, nz)),
            dma((2, NP)),
            dma((2, NP)),
            dma((CHUNKS, 2, NP)),
            dma((CHUNKS, 2, NP)),
            dma((CHUNKS, nz)),
            dma((CHUNKS, nz)),
        ],
        compiler_params=pltpu.CompilerParams(
            collective_id=0, has_side_effects=True, vmem_limit_bytes=62 << 20
        ),
    )(
        page_table,
        queries,
        kv_pool,
        ctx_lens[:, None],
        w_out.T,
        residual,
        moe_gain[None, :],
        expert_ids,
        route_weights,
        w_gate[0],
        w_up[0],
        w_down[0],
        final_gain[None, :],
    )


def solution(mesh):
    return jax.shard_map(
        shards,
        mesh=mesh,
        in_specs=(
            P("expert", "dp"),
            P(None, "expert", None, "dp"),
            P("expert", None),
            P("expert"),
            P("dp", "expert"),
            P(("expert", "dp"), None),
            P(),
            P(("expert", "dp"), None),
            P(("expert", "dp"), None),
            P("expert", "dp", None),
            P("expert", "dp", None),
            P("expert", "dp", None),
            P(),
        ),
        out_specs=P(("expert", "dp"), None),
        check_vma=False,
    )
```

```python
import functools
import math

import jax
import jax.numpy as jnp
from jax import lax
from jax.experimental import pallas as pl
from jax.experimental.pallas import tpu as pltpu
from jax.sharding import PartitionSpec as P

HD = 128
TOP = 6
CAP = 12
NP = 8
CHUNKS = 4
MESH = pl.DeviceIdType.MESH
F32 = jnp.float32
BF16 = jnp.bfloat16


def normalize(values, gain):
    mean_sq = jnp.mean(values * values, axis=-1, keepdims=True)
    return values * lax.rsqrt(mean_sq + 1e-06) * gain


def iota(shape, axis):
    return lax.broadcasted_iota(jnp.int32, shape, axis)


def dot(a, b):
    return jnp.dot(a, b, preferred_element_type=F32)


def moe_kernel(
    sizes,
    table_ref,
    q_ref,
    kv_ref,
    lens_ref,
    wot_ref,
    res_ref,
    mgain_ref,
    ids_ref,
    rw_ref,
    wg_ref,
    wu_ref,
    wd_ref,
    gain_ref,
    out_ref,
    kvs,
    lens_t,
    keys,
    vals,
    ctx,
    wo,
    prs,
    prr,
    hid,
    wgf,
    wuf,
    wdf,
    rows,
    route_out,
    route,
    snd,
    xin,
    mid,
    yout,
    ans,
    picks,
    wcomb,
    psnd,
    prcv,
    comb,
    loc_sem,
    w1_s,
    w1_r,
    w2_s,
    w2_r,
    w3_s,
    w3_r,
    pr_s,
    pr_r,
    gu_s,
    gu_r,
    wd_s,
    wd_r,
    za_s,
    za_r,
    ya_s,
    ya_r,
    ry_s,
    ry_r,
    rz_s,
    rz_r,
):
    nd, nz, order = sizes
    pos = {off: i for i, off in enumerate(order)}
    groups = 2
    per = nz // groups
    d = lax.axis_index("dp")
    e = lax.axis_index("expert")
    z = e // NP
    p = lax.rem(e, NP)
    n_rows, width = res_ref.shape
    kd = wg_ref.shape[0]
    ff = wg_ref.shape[1]
    kf = wd_ref.shape[0]
    cw = width // CHUNKS
    seg = per * CAP
    gsz = NP * seg
    right = lax.rem(d + 1, nd)
    left = lax.rem(d + nd - 1, nd)
    sends = []

    def plane(j):
        return (d, z * NP + lax.rem(p + j, NP))

    def line(off):
        return (d, lax.rem(z + off, nz) * NP + p)

    def across(k):
        return (lax.rem(d + k, nd), e)

    def remote(src, dst, s, r, to):
        c = pltpu.make_async_remote_copy(
            src_ref=src, dst_ref=dst, send_sem=s, recv_sem=r, device_id=to, device_id_type=MESH
        )
        c.start()
        sends.append(c)
        return c

    kv_c = pltpu.make_async_copy(kv_ref, kvs, loc_sem.at[4])
    kv_c.start()
    barrier = pltpu.get_barrier_semaphore()
    peers = [across(k) for k in range(1, nd)]
    peers += [line(o) for o in range(1, nz)] + [plane(j) for j in range(1, NP)]
    for peer in peers:
        pl.semaphore_signal(barrier, inc=1, device_id=peer, device_id_type=MESH)
    wo[z, p] = wot_ref[...]
    pl.semaphore_wait(barrier, len(peers))

    w1 = {}
    for off in order[1:]:
        w1[off] = remote(wot_ref, wo.at[z, p], w1_s.at[off], w1_r.at[off], line(off))

    gu = [(wg_ref, wgf), (wu_ref, wuf)]
    half = kd // 2
    gu_c = {}

    def ring_start(m):
        src, dst = gu[m]
        for side, to in ((0, right), (1, left)):
            for h in (side, 1 - side):
                gu_c[m, side, h] = remote(
                    src.at[pl.ds(h * half, half), :],
                    dst.at[pl.ds(d * kd + h * half, half), :],
                    gu_s.at[m, side, h],
                    gu_r.at[m, side, h],
                    (to, e),
                )

    ring_start(0)

    experts = nz * NP
    named = jnp.zeros((experts, n_rows), F32)
    share = jnp.zeros((experts, n_rows), F32)
    for k in range(TOP):
        hit = ids_ref[k : k + 1, :] == iota((experts, n_rows), 0)
        named = named + jnp.where(hit, 1.0, 0.0)
        share = share + jnp.where(hit, rw_ref[k : k + 1, :], 0.0)
    upper = jnp.where(iota((n_rows, n_rows), 0) < iota((n_rows, n_rows), 1), 1.0, 0.0).astype(BF16)
    rank = dot(named.astype(BF16), upper)
    rank = jnp.where(named > 0.5, rank, -1.0)
    for i in range(nz):
        route_out[i, 0:NP, :] = rank[i * NP : (i + 1) * NP, :]
        route_out[i, NP : 2 * NP, :] = share[i * NP : (i + 1) * NP, :]
    own_route = pltpu.make_async_copy(route_out.at[z], route.at[0], loc_sem.at[3])
    own_route.start()
    zr = {}
    for off in order[1:]:
        slot = pos[nz - off]
        zt = lax.rem(z + off, nz)
        zr[slot] = remote(
            route_out.at[zt], route.at[slot], za_s.at[0, off], za_r.at[0, slot], line(off)
        )

    for off in order[1:]:
        w1[off].wait_recv()
    sib = p + 1 - 2 * lax.rem(p, 2)
    sib_to = (d, z * NP + sib)
    w2 = {}
    w3 = {}
    for k in range(1, NP // 2):
        w2[k] = remote(wo.at[:, p], wo.at[:, p], w2_s.at[k], w2_r.at[k], plane(2 * k))
    w3[0] = remote(wo.at[:, p], wo.at[:, p], w3_s.at[0], w3_r.at[0], sib_to)

    seqs = table_ref.shape[0]
    pages = table_ref.shape[1]
    pool = kv_ref.shape[1]
    page = kv_ref.shape[2]
    span = pages * page
    q_rows = q_ref.shape[0] // seqs
    scale = 1.0 / math.sqrt(HD)
    lens_t[...] = jnp.transpose(jnp.broadcast_to(lens_ref[...], (128, lens_ref.shape[1])))
    kv_c.wait()

    def attend(s, carry):
        for i in range(pages):
            at = lax.rem(table_ref[s, i], pool)
            keys[i * page : (i + 1) * page, :] = kvs[0, at]
            vals[i * page : (i + 1) * page, :] = kvs[1, at]
        here = pl.ds(pl.multiple_of(s * q_rows, q_rows), q_rows)
        seen = iota((q_rows, span), 1) < lens_t[here, 0:1]
        for h in range(q_ref.shape[1] // HD):
            cols = slice(h * HD, (h + 1) * HD)
            sc = lax.dot_general(
                q_ref[here, cols], keys[:, cols], (((1,), (1,)), ((), ())), preferred_element_type=F32
            )
            sc = jnp.where(seen, sc * scale, -1e30)
            ex = jnp.where(seen, jnp.exp(sc - jnp.max(sc, axis=-1, keepdims=True)), 0.0)
            pr = (ex / jnp.sum(ex, axis=-1, keepdims=True)).astype(BF16)
            ctx[here, cols] = dot(pr, vals[:, cols]).astype(BF16)
        return carry

    lax.fori_loop(0, seqs, attend, 0)

    for k in range(1, NP // 2):
        w2[k].wait_recv()
        got = lax.rem(p + NP - 2 * k, NP)
        w3[k] = remote(wo.at[:, got], wo.at[:, got], w3_s.at[k], w3_r.at[k], sib_to)
    for k in range(NP // 2):
        w3[k].wait_recv()

    wn = NP * wot_ref.shape[0]

    def project(i, carry):
        w = wo[i].reshape(wn, wot_ref.shape[1])
        val = lax.dot_general(
            ctx[...], w, (((1,), (1,)), ((), ())), preferred_element_type=F32
        ).astype(BF16)
        cols = pl.ds(pl.multiple_of(i * wn, wn), wn)
        for j in range(nd):
            prs[j, :, cols] = val[j * n_rows : (j + 1) * n_rows, :]
        return carry

    lax.fori_loop(0, nz, project, 0)
    pr = {}
    for k in (2, 1, 3):
        pr[k] = remote(
            prs.at[lax.rem(d + k, nd)], prr.at[k], pr_s.at[k], pr_r.at[k], across(k)
        )
    ring_start(1)
    local = []
    for m, (src, dst) in enumerate(gu):
        c = pltpu.make_async_copy(src, dst.at[pl.ds(d * kd, kd), :], loc_sem.at[m])
        c.start()
        local.append(c)
    c = pltpu.make_async_copy(wd_ref, wdf.at[pl.ds(d * kf, kf), :], loc_sem.at[2])
    c.start()
    local.append(c)

    slot_i = iota((gsz, per * n_rows), 0)
    expand = jnp.where(iota((gsz, NP), 0) // seg == iota((gsz, NP), 1), 1.0, 0.0).astype(BF16)
    want = lax.rem(slot_i, CAP).astype(F32)
    block_ok = lax.rem(slot_i, seg) // CAP == iota((gsz, per * n_rows), 1) // n_rows
    for g in range(groups):
        members = range(g * per, (g + 1) * per)
        for i in members:
            if i == 0:
                own_route.wait()
            else:
                zr[i].wait_recv()
        ranks = jnp.concatenate([route[i, 0:NP, :] for i in members], axis=1)
        shares = jnp.concatenate([route[i, NP : 2 * NP, :] for i in members], axis=1)
        pick = jnp.logical_and(dot(expand, ranks.astype(BF16)) == want, block_ok)
        picks[g] = jnp.where(pick, 1.0, 0.0).astype(BF16)
        hi = shares.astype(BF16)
        lo = (shares - hi.astype(F32)).astype(BF16)
        for part, val in ((0, hi), (1, lo)):
            full = jnp.where(pick, dot(expand, val), 0.0)
            wcomb[g, part] = jnp.transpose(full).astype(BF16)

    state = res_ref[...].astype(F32) + prs[d].astype(F32)
    for k in (1, 3, 2):
        pr[k].wait_recv()
        state = state + prr[k].astype(F32)
    hid[...] = state
    rows[pl.ds(0, n_rows), :] = normalize(state, mgain_ref[...]).astype(BF16)

    far = nz // 2
    hr = n_rows // 2
    za = {}

    def hop(side, k):
        off_here = ((nz - (k - 1)) if side == 0 else (k - 1)) % nz
        off_there = (nz - k) if side == 0 else k
        src0 = pos[off_here] * n_rows
        dst0 = pos[off_there] * n_rows
        size = n_rows
        if k == far:
            size = hr
            src0 += side * hr
            dst0 += side * hr
        za[side, k] = remote(
            rows.at[pl.ds(src0, size), :],
            rows.at[pl.ds(dst0, size), :],
            za_s.at[1 + side, k],
            za_r.at[1 + side, k],
            line(1 if side == 0 else nz - 1),
        )

    def relay(k):
        for side in range(2):
            za[side, k].wait_recv()
            if k < far:
                hop(side, k + 1)

    for side in range(2):
        hop(side, 1)

    hf = kf // 2
    gu_f = {}
    wd_c = {}
    wd_f = {}

    def gu_forward(m):
        dst = gu[m][1]
        for side, frm, to in ((0, left, right), (1, right, left)):
            gu_c[m, side, side].wait_recv()
            at = pl.ds(frm * kd + side * half, half)
            gu_f[m, side] = remote(
                dst.at[at, :], dst.at[at, :], gu_s.at[m, side, 2], gu_r.at[m, side, 2], (to, e)
            )

    def wd_start(n):
        cols = pl.ds(n * cw, cw)
        for side, to in ((0, right), (1, left)):
            for h in (side, 1 - side):
                wd_c[n, side, h] = remote(
                    wd_ref.at[pl.ds(h * hf, hf), cols],
                    wdf.at[pl.ds(d * kf + h * hf, hf), cols],
                    wd_s.at[n, side, h],
                    wd_r.at[n, side, h],
                    (to, e),
                )

    def wd_forward(n):
        cols = pl.ds(n * cw, cw)
        for side, frm, to in ((0, left, right), (1, right, left)):
            wd_c[n, side, side].wait_recv()
            at = pl.ds(frm * kf + side * hf, hf)
            wd_f[n, side] = remote(
                wdf.at[at, cols], wdf.at[at, cols], wd_s.at[n, side, 2], wd_r.at[n, side, 2], (to, e)
            )

    ya = {}

    def dispatch(g):
        base = g * per * n_rows

        def tile(i, carry):
            cols = pl.ds(pl.multiple_of(i * 512, 512), 512)
            snd[g, :, cols] = dot(picks[g], rows[pl.ds(base, per * n_rows), cols]).astype(BF16)
            return carry

        lax.fori_loop(0, width // 512, tile, 0)
        for j in (4, 5, 3, 2, 6, 7, 1):
            t = lax.rem(p + j, NP)
            ya[g, j] = remote(
                snd.at[g, pl.ds(t * seg, seg), :],
                xin.at[g, pl.ds(p * seg, seg), :],
                ya_s.at[g, j],
                ya_r.at[g, j],
                plane(j),
            )
        mine = pltpu.make_async_copy(
            snd.at[g, pl.ds(p * seg, seg), :], xin.at[g, pl.ds(p * seg, seg), :], ya_s.at[g, 0]
        )
        mine.start()
        ya[g, 0] = mine

    gu_forward(0)
    for k in range(1, far // 2 + 1):
        relay(k)
    dispatch(0)
    for k in range(far // 2 + 1, far + 1):
        relay(k)
    dispatch(1)
    gu_forward(1)
    wd_start(0)
    wd_start(1)
    for m in range(2):
        local[m].wait()
        for side in range(2):
            gu_c[m, side, 1 - side].wait_recv()
            gu_f[m, side].wait_recv()

    def up_tile(g, cols):
        xs = xin[g]
        gate = dot(xs, wgf[:, cols])
        up = dot(xs, wuf[:, cols])
        mid[g, :, cols] = (gate / (1.0 + jnp.exp(-gate)) * up).astype(BF16)

    full_tiles = ff // 256
    for g in range(groups):
        for j in range(1, NP):
            ya[g, j].wait_recv()
        ya[g, 0].wait()

        def step(i, carry, g=g):
            up_tile(g, pl.ds(pl.multiple_of(i * 256, 256), 256))
            return carry

        lax.fori_loop(0, full_tiles, step, 0)
        if ff % 256:
            up_tile(g, pl.ds(full_tiles * 256, ff % 256))
        wd_forward(g)
        wd_start(g + 2)

    ry = {}
    rz = {}

    def down(n, g):
        def tile(i, carry):
            c0 = pl.multiple_of(i * 256, 256)
            val = dot(mid[g], wdf[:, pl.ds(pl.multiple_of(n * cw + i * 256, 256), 256)])
            yout[n, g, :, pl.ds(c0, 256)] = val.astype(BF16)
            return carry

        lax.fori_loop(0, cw // 256, tile, 0)
        for j in range(1, NP):
            t = lax.rem(p + j, NP)
            ry[n, g, j] = remote(
                yout.at[n, g, pl.ds(t * seg, seg), :],
                ans.at[n, g, pl.ds(p * seg, seg), :],
                ry_s.at[n, g, j],
                ry_r.at[n, g, j],
                plane(j),
            )
        mine = pltpu.make_async_copy(
            yout.at[n, g, pl.ds(p * seg, seg), :],
            ans.at[n, g, pl.ds(p * seg, seg), :],
            ry_s.at[n, g, 0],
        )
        mine.start()
        ry[n, g, 0] = mine

    def combine(n, g):
        for j in range(1, NP):
            ry[n, g, j].wait_recv()
        ry[n, g, 0].wait()
        part = dot(wcomb[g, 0], ans[n, g]) + dot(wcomb[g, 1], ans[n, g])
        psnd[n, pl.ds(g * per * n_rows, per * n_rows), :] = part.astype(BF16)
        for i in range(g * per, (g + 1) * per):
            off = order[i]
            if off == 0:
                continue
            slot = pos[nz - off]
            rz[n, slot] = remote(
                psnd.at[n, pl.ds(i * n_rows, n_rows), :],
                prcv.at[n, pl.ds(slot * n_rows, n_rows), :],
                rz_s.at[n, i],
                rz_r.at[n, slot],
                line(off),
            )

    def gather_home(n):
        total = psnd[n, 0:n_rows, :].astype(F32)
        for slot in range(1, nz):
            rz[n, slot].wait_recv()
            total = total + prcv[n, slot * n_rows : (slot + 1) * n_rows, :].astype(F32)
        cols = slice(n * cw, (n + 1) * cw)
        comb[:, cols] = hid[:, cols] + total

    local[2].wait()
    for n in range(CHUNKS):
        for side in range(2):
            wd_c[n, side, 1 - side].wait_recv()
            wd_f[n, side].wait_recv()
        for g in range(groups):
            down(n, g)
        if n + 2 < CHUNKS:
            wd_forward(n + 2)
        if n >= 1:
            for g in range(groups):
                combine(n - 1, g)
        if n >= 2:
            gather_home(n - 2)
    for g in range(groups):
        combine(CHUNKS - 1, g)
    gather_home(CHUNKS - 2)
    gather_home(CHUNKS - 1)
    out_ref[...] = normalize(comb[...], gain_ref[...]).astype(BF16)
    for c in sends:
        c.wait_send()


def shards(
    queries,
    kv_pool,
    page_table,
    ctx_lens,
    w_out,
    residual,
    moe_gain,
    expert_ids,
    route_weights,
    w_gate,
    w_up,
    w_down,
    final_gain,
):
    nd = lax.axis_size("dp")
    experts = lax.axis_size("expert")
    nz = experts // NP
    order = [0]
    for k in range(1, nz // 2 + 1):
        order.append(k)
        if nz - k != k:
            order.append(nz - k)
    n_rows, width = residual.shape
    group_rows, feats = queries.shape
    _, pool, page, _ = kv_pool.shape
    span = page_table.shape[1] * page
    wc = w_out.shape[1]
    kd, ff = w_gate.shape[1:]
    kf = w_down.shape[1]
    cw = width // CHUNKS
    per = nz // 2
    seg = per * CAP
    gsz = NP * seg
    vmem = pl.BlockSpec(memory_space=pltpu.VMEM)
    smem = pl.BlockSpec(memory_space=pltpu.SMEM)
    hbm = pl.BlockSpec(memory_space=pl.ANY)
    dma = pltpu.SemaphoreType.DMA
    return pl.pallas_call(
        functools.partial(moe_kernel, (nd, nz, order)),
        out_shape=jax.ShapeDtypeStruct((n_rows, width), BF16),
        in_specs=[smem, vmem, hbm, vmem, vmem, vmem, vmem, vmem, vmem, hbm, hbm, hbm, vmem],
        out_specs=vmem,
        scratch_shapes=[
            pltpu.VMEM((2, pool, page, feats), BF16),
            pltpu.VMEM((group_rows, 128), jnp.int32),
            pltpu.VMEM((span, feats), BF16),
            pltpu.VMEM((span, feats), BF16),
            pltpu.VMEM((group_rows, feats), BF16),
            pltpu.VMEM((nz, NP, wc, feats), BF16),
            pltpu.VMEM((nd, n_rows, width), BF16),
            pltpu.VMEM((nd, n_rows, width), BF16),
            pltpu.VMEM((n_rows, width), F32),
            pltpu.VMEM((nd * kd, ff), BF16),
            pltpu.VMEM((nd * kd, ff), BF16),
            pltpu.VMEM((nd * kf, width), BF16),
            pltpu.VMEM((nz * n_rows, width), BF16),
            pltpu.VMEM((nz, 2 * NP, n_rows), F32),
            pltpu.VMEM((nz, 2 * NP, n_rows), F32),
            pltpu.VMEM((2, gsz, width), BF16),
            pltpu.VMEM((2, gsz, width), BF16),
            pltpu.VMEM((2, gsz, ff), BF16),
            pltpu.VMEM((CHUNKS, 2, gsz, cw), BF16),
            pltpu.VMEM((CHUNKS, 2, gsz, cw), BF16),
            pltpu.VMEM((2, gsz, per * n_rows), BF16),
            pltpu.VMEM((2, 2, per * n_rows, gsz), BF16),
            pltpu.VMEM((CHUNKS, nz * n_rows, cw), BF16),
            pltpu.VMEM((CHUNKS, nz * n_rows, cw), BF16),
            pltpu.VMEM((n_rows, width), F32),
            dma((5,)),
            dma((nz,)),
            dma((nz,)),
            dma((NP // 2,)),
            dma((NP // 2,)),
            dma((NP // 2,)),
            dma((NP // 2,)),
            dma((nd,)),
            dma((nd,)),
            dma((2, 2, 3)),
            dma((2, 2, 3)),
            dma((CHUNKS, 2, 3)),
            dma((CHUNKS, 2, 3)),
            dma((3, nz)),
            dma((3, nz)),
            dma((2, NP)),
            dma((2, NP)),
            dma((CHUNKS, 2, NP)),
            dma((CHUNKS, 2, NP)),
            dma((CHUNKS, nz)),
            dma((CHUNKS, nz)),
        ],
        compiler_params=pltpu.CompilerParams(
            collective_id=0, has_side_effects=True, vmem_limit_bytes=62 << 20
        ),
    )(
        page_table,
        queries,
        kv_pool,
        ctx_lens[None, :],
        w_out.T,
        residual,
        moe_gain[None, :],
        expert_ids.T,
        route_weights.T,
        w_gate[0],
        w_up[0],
        w_down[0],
        final_gain[None, :],
    )


def solution(mesh):
    return jax.shard_map(
        shards,
        mesh=mesh,
        in_specs=(
            P("expert", "dp"),
            P(None, "expert", None, "dp"),
            P("expert", None),
            P("expert"),
            P("dp", "expert"),
            P(("expert", "dp"), None),
            P(),
            P(("expert", "dp"), None),
            P(("expert", "dp"), None),
            P("expert", "dp", None),
            P("expert", "dp", None),
            P("expert", "dp", None),
            P(),
        ),
        out_specs=P(("expert", "dp"), None),
        check_vma=False,
    )
```

```python
import functools
import math

import jax
import jax.numpy as jnp
from jax import lax
from jax.experimental import pallas as pl
from jax.experimental.pallas import tpu as pltpu
from jax.sharding import PartitionSpec as P

HD = 128
TOP = 6
CAP = 12
NP = 8
WIDTHS = (256, 384, 384, 384, 256, 256, 128)
STARTS = (0, 256, 640, 1024, 1408, 1664, 1920)
CHUNKS = 7
MESH = pl.DeviceIdType.MESH
F32 = jnp.float32
BF16 = jnp.bfloat16


def normalize(values, gain):
    mean_sq = jnp.mean(values * values, axis=-1, keepdims=True)
    return values * lax.rsqrt(mean_sq + 1e-06) * gain


def iota(shape, axis):
    return lax.broadcasted_iota(jnp.int32, shape, axis)


def dot(a, b):
    return jnp.dot(a, b, preferred_element_type=F32)


def moe_kernel(
    sizes,
    table_ref,
    q_ref,
    kv_ref,
    lens_ref,
    wot_ref,
    res_ref,
    mgain_ref,
    ids_ref,
    rw_ref,
    wg_ref,
    wu_ref,
    wd_ref,
    gain_ref,
    out_ref,
    kvs,
    lens_t,
    keys,
    vals,
    ctx,
    wo,
    prs,
    prr,
    hid,
    wgf,
    wuf,
    wdf,
    rows,
    route_out,
    route,
    snd,
    xin,
    mid,
    yout,
    ans,
    picks,
    wcomb,
    psnd,
    prcv,
    comb,
    loc_sem,
    w1_s,
    w1_r,
    w2_s,
    w2_r,
    w3_s,
    w3_r,
    pr_s,
    pr_r,
    gu_s,
    gu_r,
    wd_s,
    wd_r,
    za_s,
    za_r,
    ya_s,
    ya_r,
    ry_s,
    ry_r,
    rz_s,
    rz_r,
):
    nd, nz, order = sizes
    pos = {off: i for i, off in enumerate(order)}
    groups = 2
    per = nz // groups
    d = lax.axis_index("dp")
    e = lax.axis_index("expert")
    z = e // NP
    p = lax.rem(e, NP)
    n_rows, width = res_ref.shape
    kd = wg_ref.shape[0]
    ff = wg_ref.shape[1]
    kf = wd_ref.shape[0]
    seg = per * CAP
    gsz = NP * seg
    right = lax.rem(d + 1, nd)
    left = lax.rem(d + nd - 1, nd)
    sends = []

    def plane(j):
        return (d, z * NP + lax.rem(p + j, NP))

    def line(off):
        return (d, lax.rem(z + off, nz) * NP + p)

    def across(k):
        return (lax.rem(d + k, nd), e)

    def remote(src, dst, s, r, to):
        c = pltpu.make_async_remote_copy(
            src_ref=src, dst_ref=dst, send_sem=s, recv_sem=r, device_id=to, device_id_type=MESH
        )
        c.start()
        sends.append(c)
        return c

    kv_c = pltpu.make_async_copy(kv_ref, kvs, loc_sem.at[4])
    kv_c.start()
    barrier = pltpu.get_barrier_semaphore()
    peers = [across(k) for k in range(1, nd)]
    peers += [line(o) for o in range(1, nz)] + [plane(j) for j in range(1, NP)]
    for peer in peers:
        pl.semaphore_signal(barrier, inc=1, device_id=peer, device_id_type=MESH)
    wo[z, p] = wot_ref[...]
    pl.semaphore_wait(barrier, len(peers))

    w1 = {}
    for off in order[1:]:
        w1[off] = remote(wot_ref, wo.at[z, p], w1_s.at[off], w1_r.at[off], line(off))

    gu = [(wg_ref, wgf), (wu_ref, wuf)]
    half = kd // 2
    gu_c = {}

    parts = ((0, 512), (512, 512), (1024, ff - 1024))
    cut = 6 * 128

    def ring_start(m, goes_on, i=0, c0=0, cn=ff):
        src, dst = gu[m]
        for side, to in ((0, right), (1, left)):
            h = side if goes_on else 1 - side
            gu_c[m, side, h, i] = remote(
                src.at[pl.ds(h * half, half), pl.ds(c0, cn)],
                dst.at[pl.ds(d * kd + h * half, half), pl.ds(c0, cn)],
                gu_s.at[m, side, h + i],
                gu_r.at[m, side, h + i],
                (to, e),
            )

    ring_start(0, True)
    ring_start(0, False, 0, 0, cut)

    experts = nz * NP
    named = jnp.zeros((experts, n_rows), F32)
    share = jnp.zeros((experts, n_rows), F32)
    for k in range(TOP):
        hit = ids_ref[k : k + 1, :] == iota((experts, n_rows), 0)
        named = named + jnp.where(hit, 1.0, 0.0)
        share = share + jnp.where(hit, rw_ref[k : k + 1, :], 0.0)
    upper = jnp.where(iota((n_rows, n_rows), 0) < iota((n_rows, n_rows), 1), 1.0, 0.0).astype(BF16)
    rank = dot(named.astype(BF16), upper)
    rank = jnp.where(named > 0.5, rank, -1.0)
    for i in range(nz):
        route_out[i, 0:NP, :] = rank[i * NP : (i + 1) * NP, :]
        route_out[i, NP : 2 * NP, :] = share[i * NP : (i + 1) * NP, :]
    own_route = pltpu.make_async_copy(route_out.at[z], route.at[0], loc_sem.at[3])
    own_route.start()
    zr = {}
    for off in order[1:]:
        slot = pos[nz - off]
        zt = lax.rem(z + off, nz)
        zr[slot] = remote(
            route_out.at[zt], route.at[slot], za_s.at[0, off], za_r.at[0, slot], line(off)
        )

    for off in order[1:]:
        w1[off].wait_recv()
    sib = p + 1 - 2 * lax.rem(p, 2)
    sib_to = (d, z * NP + sib)
    w2 = {}
    w3 = {}
    for k in range(1, NP // 2):
        w2[k] = remote(wo.at[:, p], wo.at[:, p], w2_s.at[k], w2_r.at[k], plane(2 * k))
    w3[0] = remote(wo.at[:, p], wo.at[:, p], w3_s.at[0], w3_r.at[0], sib_to)

    seqs = table_ref.shape[0]
    pages = table_ref.shape[1]
    pool = kv_ref.shape[1]
    page = kv_ref.shape[2]
    span = pages * page
    q_rows = q_ref.shape[0] // seqs
    scale = 1.0 / math.sqrt(HD)
    lens_t[...] = jnp.transpose(jnp.broadcast_to(lens_ref[...], (128, lens_ref.shape[1])))
    kv_c.wait()

    def attend(s, carry):
        for i in range(pages):
            at = lax.rem(table_ref[s, i], pool)
            keys[i * page : (i + 1) * page, :] = kvs[0, at]
            vals[i * page : (i + 1) * page, :] = kvs[1, at]
        here = pl.ds(pl.multiple_of(s * q_rows, q_rows), q_rows)
        seen = iota((q_rows, span), 1) < lens_t[here, 0:1]
        for h in range(q_ref.shape[1] // HD):
            cols = slice(h * HD, (h + 1) * HD)
            sc = lax.dot_general(
                q_ref[here, cols], keys[:, cols], (((1,), (1,)), ((), ())), preferred_element_type=F32
            )
            sc = jnp.where(seen, sc * scale, -1e30)
            ex = jnp.where(seen, jnp.exp(sc - jnp.max(sc, axis=-1, keepdims=True)), 0.0)
            pr = (ex / jnp.sum(ex, axis=-1, keepdims=True)).astype(BF16)
            ctx[here, cols] = dot(pr, vals[:, cols]).astype(BF16)
        return carry

    lax.fori_loop(0, seqs, attend, 0)

    for k in range(1, NP // 2):
        w2[k].wait_recv()
        got = lax.rem(p + NP - 2 * k, NP)
        w3[k] = remote(wo.at[:, got], wo.at[:, got], w3_s.at[k], w3_r.at[k], sib_to)
    for k in range(NP // 2):
        w3[k].wait_recv()

    wn = NP * wot_ref.shape[0]

    def project(i, carry):
        w = wo[i].reshape(wn, wot_ref.shape[1])
        val = lax.dot_general(
            ctx[...], w, (((1,), (1,)), ((), ())), preferred_element_type=F32
        ).astype(BF16)
        cols = pl.ds(pl.multiple_of(i * wn, wn), wn)
        for j in range(nd):
            prs[j, :, cols] = val[j * n_rows : (j + 1) * n_rows, :]
        return carry

    lax.fori_loop(0, nz, project, 0)
    pr = {}
    for k in (2, 1, 3):
        pr[k] = remote(
            prs.at[lax.rem(d + k, nd)], prr.at[k], pr_s.at[k], pr_r.at[k], across(k)
        )
    ring_start(0, False, 2, cut, ff - cut)
    ring_start(1, True)
    ring_start(1, False)
    local = []
    for m, (src, dst) in enumerate(gu):
        c = pltpu.make_async_copy(src, dst.at[pl.ds(d * kd, kd), :], loc_sem.at[m])
        c.start()
        local.append(c)
    c = pltpu.make_async_copy(wd_ref, wdf.at[pl.ds(d * kf, kf), :], loc_sem.at[2])
    c.start()
    local.append(c)

    slot_i = iota((gsz, per * n_rows), 0)
    expand = jnp.where(iota((gsz, NP), 0) // seg == iota((gsz, NP), 1), 1.0, 0.0).astype(BF16)
    want = lax.rem(slot_i, CAP).astype(F32)
    block_ok = lax.rem(slot_i, seg) // CAP == iota((gsz, per * n_rows), 1) // n_rows
    for g in range(groups):
        members = range(g * per, (g + 1) * per)
        for i in members:
            if i == 0:
                own_route.wait()
            else:
                zr[i].wait_recv()
        ranks = jnp.concatenate([route[i, 0:NP, :] for i in members], axis=1)
        shares = jnp.concatenate([route[i, NP : 2 * NP, :] for i in members], axis=1)
        pick = jnp.logical_and(dot(expand, ranks.astype(BF16)) == want, block_ok)
        picks[g] = jnp.where(pick, 1.0, 0.0).astype(BF16)
        hi = shares.astype(BF16)
        lo = (shares - hi.astype(F32)).astype(BF16)
        for part, val in ((0, hi), (1, lo)):
            full = jnp.where(pick, dot(expand, val), 0.0)
            wcomb[g, part] = jnp.transpose(full).astype(BF16)

    state = res_ref[...].astype(F32) + prs[d].astype(F32)
    for k in (1, 3, 2):
        pr[k].wait_recv()
        state = state + prr[k].astype(F32)
    hid[...] = state
    rows[pl.ds(0, n_rows), :] = normalize(state, mgain_ref[...]).astype(BF16)

    far = nz // 2
    hr = n_rows // 2
    za = {}

    def hop(side, k):
        off_here = ((nz - (k - 1)) if side == 0 else (k - 1)) % nz
        off_there = (nz - k) if side == 0 else k
        src0 = pos[off_here] * n_rows
        dst0 = pos[off_there] * n_rows
        size = n_rows
        if k == far:
            size = hr
            src0 += side * hr
            dst0 += side * hr
        za[side, k] = remote(
            rows.at[pl.ds(src0, size), :],
            rows.at[pl.ds(dst0, size), :],
            za_s.at[1 + side, k],
            za_r.at[1 + side, k],
            line(1 if side == 0 else nz - 1),
        )

    def relay(k):
        for side in range(2):
            za[side, k].wait_recv()
            if k < far:
                hop(side, k + 1)

    for side in range(2):
        hop(side, 1)

    hf = kf // 2
    gu_f = {}
    wd_c = {}
    wd_f = {}

    def gu_forward():
        for m in range(2):
            for side in range(2):
                gu_c[m, side, side, 0].wait_recv()
        for i, (c0, cn) in enumerate(parts):
            for m in range(2):
                dst = gu[m][1]
                for side, frm, to in ((0, left, right), (1, right, left)):
                    at = pl.ds(frm * kd + side * half, half)
                    gu_f[m, side, i] = remote(
                        dst.at[at, pl.ds(c0, cn)],
                        dst.at[at, pl.ds(c0, cn)],
                        gu_s.at[m, side, 4 + i],
                        gu_r.at[m, side, 4 + i],
                        (to, e),
                    )

    def wd_start(n, goes_on):
        cols = pl.ds(STARTS[n], WIDTHS[n])
        for side, to in ((0, right), (1, left)):
            h = side if goes_on else 1 - side
            wd_c[n, side, h] = remote(
                wd_ref.at[pl.ds(h * hf, hf), cols],
                wdf.at[pl.ds(d * kf + h * hf, hf), cols],
                wd_s.at[n, side, h],
                wd_r.at[n, side, h],
                (to, e),
            )

    def wd_forward(n):
        cols = pl.ds(STARTS[n], WIDTHS[n])
        for side, frm, to in ((0, left, right), (1, right, left)):
            wd_c[n, side, side].wait_recv()
            at = pl.ds(frm * kf + side * hf, hf)
            wd_f[n, side] = remote(
                wdf.at[at, cols], wdf.at[at, cols], wd_s.at[n, side, 2], wd_r.at[n, side, 2], (to, e)
            )

    def wd_next(n):
        if n < CHUNKS:
            wd_forward(n)
            wd_start(n, False)
        if n + 2 < CHUNKS:
            wd_start(n + 2, True)

    ya = {}

    def dispatch(g):
        base = g * per * n_rows

        def tile(i, carry):
            cols = pl.ds(pl.multiple_of(i * 512, 512), 512)
            snd[g, :, cols] = dot(picks[g], rows[pl.ds(base, per * n_rows), cols]).astype(BF16)
            return carry

        lax.fori_loop(0, width // 512, tile, 0)
        for j in (4, 5, 3, 2, 6, 7, 1):
            t = lax.rem(p + j, NP)
            ya[g, j] = remote(
                snd.at[g, pl.ds(t * seg, seg), :],
                xin.at[g, pl.ds(p * seg, seg), :],
                ya_s.at[g, j],
                ya_r.at[g, j],
                plane(j),
            )
        mine = pltpu.make_async_copy(
            snd.at[g, pl.ds(p * seg, seg), :], xin.at[g, pl.ds(p * seg, seg), :], ya_s.at[g, 0]
        )
        mine.start()
        ya[g, 0] = mine

    for k in range(1, far // 2 + 1):
        relay(k)
    dispatch(0)
    relay(far // 2 + 1)
    gu_forward()
    for k in range(far // 2 + 2, far + 1):
        relay(k)
    dispatch(1)
    wd_start(0, True)
    wd_start(1, True)
    for m in range(2):
        local[m].wait()
    for side in range(2):
        gu_c[0, side, 1 - side, 2].wait_recv()
    for m in range(2):
        for side in range(2):
            gu_c[m, side, 1 - side, 0].wait_recv()

    def up_tile(g, cols):
        xs = xin[g]
        gate = dot(xs, wgf[:, cols])
        up = dot(xs, wuf[:, cols])
        mid[g, :, cols] = (gate / (1.0 + jnp.exp(-gate)) * up).astype(BF16)

    for i, (c0, cn) in enumerate(parts):
        for m in range(2):
            for side in range(2):
                gu_f[m, side, i].wait_recv()
        for g in range(groups):
            if i == 0:
                for j in range(1, NP):
                    ya[g, j].wait_recv()
                ya[g, 0].wait()

            def step(t, carry, g=g, c0=c0):
                up_tile(g, pl.ds(pl.multiple_of(c0 + t * 256, 256), 256))
                return carry

            lax.fori_loop(0, cn // 256, step, 0)
            if cn % 256:
                up_tile(g, pl.ds(c0 + cn // 256 * 256, cn % 256))

    ry = {}
    rz = {}

    def down(n):
        def tile(g, c0, cn):
            cols = pl.ds(c0, cn)
            yout[g, :, cols] = dot(mid[g], wdf[:, cols]).astype(BF16)

        for g in range(groups):
            for c in range(0, WIDTHS[n], 256):
                tile(g, STARTS[n] + c, min(256, WIDTHS[n] - c))
        cols = pl.ds(STARTS[n], WIDTHS[n])
        for j in (4, 5, 3, 2, 6, 7, 1):
            t = lax.rem(p + j, NP)
            ry[n, j] = remote(
                yout.at[:, pl.ds(t * seg, seg), cols],
                ans.at[:, pl.ds(p * seg, seg), cols],
                ry_s.at[n, j],
                ry_r.at[n, j],
                plane(j),
            )
        mine = pltpu.make_async_copy(
            yout.at[:, pl.ds(p * seg, seg), cols],
            ans.at[:, pl.ds(p * seg, seg), cols],
            ry_s.at[n, 0],
        )
        mine.start()
        ry[n, 0] = mine

    def combine(n):
        cols = pl.ds(STARTS[n], WIDTHS[n])
        for j in range(1, NP):
            ry[n, j].wait_recv()
        ry[n, 0].wait()
        for g in (1, 0):
            part = dot(wcomb[g, 0], ans[g, :, cols]) + dot(wcomb[g, 1], ans[g, :, cols])
            psnd[g * per * n_rows : (g + 1) * per * n_rows, cols] = part.astype(BF16)
            for i in range((g + 1) * per - 1, g * per - 1, -1):
                off = order[i]
                if off == 0:
                    continue
                slot = pos[nz - off]
                rz[n, slot] = remote(
                    psnd.at[pl.ds(i * n_rows, n_rows), cols],
                    prcv.at[pl.ds(slot * n_rows, n_rows), cols],
                    rz_s.at[n, i],
                    rz_r.at[n, slot],
                    line(off),
                )

    def gather_home(n):
        cols = slice(STARTS[n], STARTS[n] + WIDTHS[n])
        total = psnd[0:n_rows, cols].astype(F32)
        for slot in range(1, nz):
            rz[n, slot].wait_recv()
            total = total + prcv[slot * n_rows : (slot + 1) * n_rows, cols].astype(F32)
        comb[:, cols] = hid[:, cols] + total

    wd_next(0)
    wd_next(1)
    local[2].wait()
    for n in range(CHUNKS):
        for side in range(2):
            wd_c[n, side, 1 - side].wait_recv()
            wd_f[n, side].wait_recv()
        down(n)
        if n >= 1:
            combine(n - 1)
        wd_next(n + 2)
        if n >= 3:
            gather_home(n - 3)
    combine(CHUNKS - 1)
    gather_home(CHUNKS - 3)
    gather_home(CHUNKS - 2)
    gather_home(CHUNKS - 1)
    out_ref[...] = normalize(comb[...], gain_ref[...]).astype(BF16)
    for c in sends:
        c.wait_send()


def shards(
    queries,
    kv_pool,
    page_table,
    ctx_lens,
    w_out,
    residual,
    moe_gain,
    expert_ids,
    route_weights,
    w_gate,
    w_up,
    w_down,
    final_gain,
):
    nd = lax.axis_size("dp")
    experts = lax.axis_size("expert")
    nz = experts // NP
    order = [0]
    for k in range(1, nz // 2 + 1):
        order.append(k)
        if nz - k != k:
            order.append(nz - k)
    n_rows, width = residual.shape
    group_rows, feats = queries.shape
    _, pool, page, _ = kv_pool.shape
    span = page_table.shape[1] * page
    wc = w_out.shape[1]
    kd, ff = w_gate.shape[1:]
    kf = w_down.shape[1]
    per = nz // 2
    seg = per * CAP
    gsz = NP * seg
    vmem = pl.BlockSpec(memory_space=pltpu.VMEM)
    smem = pl.BlockSpec(memory_space=pltpu.SMEM)
    hbm = pl.BlockSpec(memory_space=pl.ANY)
    dma = pltpu.SemaphoreType.DMA
    return pl.pallas_call(
        functools.partial(moe_kernel, (nd, nz, order)),
        out_shape=jax.ShapeDtypeStruct((n_rows, width), BF16),
        in_specs=[smem, vmem, hbm, vmem, vmem, vmem, vmem, vmem, vmem, hbm, hbm, hbm, vmem],
        out_specs=vmem,
        scratch_shapes=[
            pltpu.VMEM((2, pool, page, feats), BF16),
            pltpu.VMEM((group_rows, 128), jnp.int32),
            pltpu.VMEM((span, feats), BF16),
            pltpu.VMEM((span, feats), BF16),
            pltpu.VMEM((group_rows, feats), BF16),
            pltpu.VMEM((nz, NP, wc, feats), BF16),
            pltpu.VMEM((nd, n_rows, width), BF16),
            pltpu.VMEM((nd, n_rows, width), BF16),
            pltpu.VMEM((n_rows, width), F32),
            pltpu.VMEM((nd * kd, ff), BF16),
            pltpu.VMEM((nd * kd, ff), BF16),
            pltpu.VMEM((nd * kf, width), BF16),
            pltpu.VMEM((nz * n_rows, width), BF16),
            pltpu.VMEM((nz, 2 * NP, n_rows), F32),
            pltpu.VMEM((nz, 2 * NP, n_rows), F32),
            pltpu.VMEM((2, gsz, width), BF16),
            pltpu.VMEM((2, gsz, width), BF16),
            pltpu.VMEM((2, gsz, ff), BF16),
            pltpu.VMEM((2, gsz, width), BF16),
            pltpu.VMEM((2, gsz, width), BF16),
            pltpu.VMEM((2, gsz, per * n_rows), BF16),
            pltpu.VMEM((2, 2, per * n_rows, gsz), BF16),
            pltpu.VMEM((nz * n_rows, width), BF16),
            pltpu.VMEM((nz * n_rows, width), BF16),
            pltpu.VMEM((n_rows, width), F32),
            dma((5,)),
            dma((nz,)),
            dma((nz,)),
            dma((NP // 2,)),
            dma((NP // 2,)),
            dma((NP // 2,)),
            dma((NP // 2,)),
            dma((nd,)),
            dma((nd,)),
            dma((2, 2, 7)),
            dma((2, 2, 7)),
            dma((CHUNKS, 2, 3)),
            dma((CHUNKS, 2, 3)),
            dma((3, nz)),
            dma((3, nz)),
            dma((2, NP)),
            dma((2, NP)),
            dma((CHUNKS, NP)),
            dma((CHUNKS, NP)),
            dma((CHUNKS, nz)),
            dma((CHUNKS, nz)),
        ],
        compiler_params=pltpu.CompilerParams(
            collective_id=0, has_side_effects=True, vmem_limit_bytes=62 << 20
        ),
    )(
        page_table,
        queries,
        kv_pool,
        ctx_lens[None, :],
        w_out.T,
        residual,
        moe_gain[None, :],
        expert_ids.T,
        route_weights.T,
        w_gate[0],
        w_up[0],
        w_down[0],
        final_gain[None, :],
    )


def solution(mesh):
    return jax.shard_map(
        shards,
        mesh=mesh,
        in_specs=(
            P("expert", "dp"),
            P(None, "expert", None, "dp"),
            P("expert", None),
            P("expert"),
            P("dp", "expert"),
            P(("expert", "dp"), None),
            P(),
            P(("expert", "dp"), None),
            P(("expert", "dp"), None),
            P("expert", "dp", None),
            P("expert", "dp", None),
            P("expert", "dp", None),
            P(),
        ),
        out_specs=P(("expert", "dp"), None),
        check_vma=False,
    )
```

```python
import functools
import math

import jax
import jax.numpy as jnp
from jax import lax
from jax.experimental import pallas as pl
from jax.experimental.pallas import tpu as pltpu
from jax.sharding import PartitionSpec as P

HD = 128
TOP = 6
CAP = 12
NP = 8
WIDTHS = (256, 384, 384, 384, 256, 256, 128)
STARTS = (0, 256, 640, 1024, 1408, 1664, 1920)
CHUNKS = 7
MESH = pl.DeviceIdType.MESH
F32 = jnp.float32
BF16 = jnp.bfloat16


def normalize(values, gain):
    mean_sq = jnp.mean(values * values, axis=-1, keepdims=True)
    return values * lax.rsqrt(mean_sq + 1e-06) * gain


def iota(shape, axis):
    return lax.broadcasted_iota(jnp.int32, shape, axis)


def dot(a, b):
    return jnp.dot(a, b, preferred_element_type=F32)


def moe_kernel(
    sizes,
    table_ref,
    q_ref,
    kv_ref,
    lens_ref,
    wot_ref,
    res_ref,
    mgain_ref,
    ids_ref,
    rw_ref,
    wg_ref,
    wu_ref,
    wd_ref,
    gain_ref,
    out_ref,
    kvs,
    lens_t,
    keys,
    vals,
    ctx,
    wo,
    prs,
    prr,
    hid,
    wgf,
    wuf,
    wdf,
    rows,
    route_out,
    route,
    snd,
    xin,
    mid,
    yout,
    ans,
    picks,
    wcomb,
    psnd,
    parta,
    partb,
    partc,
    comb,
    loc_sem,
    w1_s,
    w1_r,
    w2_s,
    w2_r,
    w3_s,
    w3_r,
    pr_s,
    pr_r,
    gu_s,
    gu_r,
    wd_s,
    wd_r,
    za_s,
    za_r,
    ya_s,
    ya_r,
    ry_s,
    ry_r,
    rz_s,
    rz_r,
    rd_s,
    rd_r,
):
    nd, nz, order = sizes
    pos = {off: i for i, off in enumerate(order)}
    groups = 2
    per = nz // groups
    d = lax.axis_index("dp")
    e = lax.axis_index("expert")
    z = e // NP
    p = lax.rem(e, NP)
    n_rows, width = res_ref.shape
    kd = wg_ref.shape[0]
    ff = wg_ref.shape[1]
    kf = wd_ref.shape[0]
    seg = per * CAP
    gsz = NP * seg
    right = lax.rem(d + 1, nd)
    left = lax.rem(d + nd - 1, nd)
    sends = []

    def plane(j):
        return (d, z * NP + lax.rem(p + j, NP))

    def line(off):
        return (d, lax.rem(z + off, nz) * NP + p)

    def remote(src, dst, s, r, to):
        c = pltpu.make_async_remote_copy(
            src_ref=src, dst_ref=dst, send_sem=s, recv_sem=r, device_id=to, device_id_type=MESH
        )
        c.start()
        sends.append(c)
        return c

    kv_c = pltpu.make_async_copy(kv_ref, kvs, loc_sem.at[4])
    kv_c.start()
    barrier = pltpu.get_barrier_semaphore()
    peers = [(right, e), (left, e)]
    peers += [line(o) for o in range(1, nz)] + [plane(j) for j in range(1, NP)]
    for peer in peers:
        pl.semaphore_signal(barrier, inc=1, device_id=peer, device_id_type=MESH)
    wo[z, p] = wot_ref[...]
    pl.semaphore_wait(barrier, len(peers))

    gu = [(wg_ref, wgf), (wu_ref, wuf)]
    half = kd // 2
    gu_c = {}

    parts = ((0, 512), (512, 512), (1024, ff - 1024))
    cut = 6 * 128

    def ring_start(m, goes_on, i=0, c0=0, cn=ff):
        src, dst = gu[m]
        for side, to in ((0, right), (1, left)):
            h = side if goes_on else 1 - side
            gu_c[m, side, h, i] = remote(
                src.at[pl.ds(h * half, half), pl.ds(c0, cn)],
                dst.at[pl.ds(d * kd + h * half, half), pl.ds(c0, cn)],
                gu_s.at[m, side, h + i],
                gu_r.at[m, side, h + i],
                (to, e),
            )

    ring_start(0, True)

    w1 = {}
    for off in order[1:]:
        w1[off] = remote(wot_ref, wo.at[z, p], w1_s.at[off], w1_r.at[off], line(off))
    ring_start(0, False, 0, 0, cut)

    experts = nz * NP
    named = jnp.zeros((experts, n_rows), F32)
    share = jnp.zeros((experts, n_rows), F32)
    for k in range(TOP):
        hit = ids_ref[k : k + 1, :] == iota((experts, n_rows), 0)
        named = named + jnp.where(hit, 1.0, 0.0)
        share = share + jnp.where(hit, rw_ref[k : k + 1, :], 0.0)
    upper = jnp.where(iota((n_rows, n_rows), 0) < iota((n_rows, n_rows), 1), 1.0, 0.0).astype(BF16)
    rank = dot(named.astype(BF16), upper)
    rank = jnp.where(named > 0.5, rank, -1.0)
    for i in range(nz):
        route_out[i, 0:NP, :] = rank[i * NP : (i + 1) * NP, :]
        route_out[i, NP : 2 * NP, :] = share[i * NP : (i + 1) * NP, :]
    own_route = pltpu.make_async_copy(route_out.at[z], route.at[0], loc_sem.at[3])
    own_route.start()
    zr = {}
    for off in order[1:]:
        slot = pos[nz - off]
        zt = lax.rem(z + off, nz)
        zr[slot] = remote(
            route_out.at[zt], route.at[slot], za_s.at[0, off], za_r.at[0, slot], line(off)
        )

    for off in order[1:]:
        w1[off].wait_recv()
    sib = p + 1 - 2 * lax.rem(p, 2)
    sib_to = (d, z * NP + sib)
    w2 = {}
    w3 = {}
    for k in range(1, NP // 2):
        w2[k] = remote(wo.at[:, p], wo.at[:, p], w2_s.at[k], w2_r.at[k], plane(2 * k))
    w3[0] = remote(wo.at[:, p], wo.at[:, p], w3_s.at[0], w3_r.at[0], sib_to)

    seqs = table_ref.shape[0]
    pages = table_ref.shape[1]
    pool = kv_ref.shape[1]
    page = kv_ref.shape[2]
    span = pages * page
    q_rows = q_ref.shape[0] // seqs
    scale = 1.0 / math.sqrt(HD)
    lens_t[...] = jnp.transpose(jnp.broadcast_to(lens_ref[...], (128, lens_ref.shape[1])))
    kv_c.wait()

    def attend(s, carry):
        for i in range(pages):
            at = lax.rem(table_ref[s, i], pool)
            keys[i * page : (i + 1) * page, :] = kvs[0, at]
            vals[i * page : (i + 1) * page, :] = kvs[1, at]
        here = pl.ds(pl.multiple_of(s * q_rows, q_rows), q_rows)
        seen = iota((q_rows, span), 1) < lens_t[here, 0:1]
        for h in range(q_ref.shape[1] // HD):
            cols = slice(h * HD, (h + 1) * HD)
            sc = lax.dot_general(
                q_ref[here, cols], keys[:, cols], (((1,), (1,)), ((), ())), preferred_element_type=F32
            )
            sc = jnp.where(seen, sc * scale, -1e30)
            ex = jnp.where(seen, jnp.exp(sc - jnp.max(sc, axis=-1, keepdims=True)), 0.0)
            pr = (ex / jnp.sum(ex, axis=-1, keepdims=True)).astype(BF16)
            ctx[here, cols] = dot(pr, vals[:, cols]).astype(BF16)
        return carry

    lax.fori_loop(0, seqs, attend, 0)

    for k in range(1, NP // 2):
        w2[k].wait_recv()
        got = lax.rem(p + NP - 2 * k, NP)
        w3[k] = remote(wo.at[:, got], wo.at[:, got], w3_s.at[k], w3_r.at[k], sib_to)
    for k in range(NP // 2):
        w3[k].wait_recv()

    wn = NP * wot_ref.shape[0]

    def project(i, carry):
        w = wo[i].reshape(wn, wot_ref.shape[1])
        val = lax.dot_general(
            ctx[...], w, (((1,), (1,)), ((), ())), preferred_element_type=F32
        ).astype(BF16)
        cols = pl.ds(pl.multiple_of(i * wn, wn), wn)
        for j in range(nd):
            prs[j, :, cols] = val[j * n_rows : (j + 1) * n_rows, :]
        return carry

    lax.fori_loop(0, nz, project, 0)
    pr = {}
    hw = width // 2
    opposite = lax.rem(d + 2, nd)
    for side, to in ((0, right), (1, left)):
        cols = pl.ds(side * hw, hw)
        pr[side] = remote(
            prs.at[opposite, :, cols],
            prr.at[2, :, cols],
            pr_s.at[side],
            pr_r.at[side],
            (to, e),
        )
    ring_start(0, False, 2, cut, ff - cut)
    for side, to in ((0, right), (1, left)):
        pr[side].wait_recv()
        cols = slice(side * hw, (side + 1) * hw)
        prs[to, :, cols] = (prs[to, :, cols].astype(F32) + prr[2, :, cols].astype(F32)).astype(BF16)
        pr[2 + side] = remote(
            prs.at[to], prr.at[side], pr_s.at[2 + side], pr_r.at[2 + side], (to, e)
        )
    ring_start(1, True)
    ring_start(1, False)
    local = []
    for m, (src, dst) in enumerate(gu):
        c = pltpu.make_async_copy(src, dst.at[pl.ds(d * kd, kd), :], loc_sem.at[m])
        c.start()
        local.append(c)
    c = pltpu.make_async_copy(wd_ref, wdf.at[pl.ds(d * kf, kf), :], loc_sem.at[2])
    c.start()
    local.append(c)

    slot_i = iota((gsz, per * n_rows), 0)
    expand = jnp.where(iota((gsz, NP), 0) // seg == iota((gsz, NP), 1), 1.0, 0.0).astype(BF16)
    want = lax.rem(slot_i, CAP).astype(F32)
    block_ok = lax.rem(slot_i, seg) // CAP == iota((gsz, per * n_rows), 1) // n_rows
    for g in range(groups):
        members = range(g * per, (g + 1) * per)
        for i in members:
            if i == 0:
                own_route.wait()
            else:
                zr[i].wait_recv()
        ranks = jnp.concatenate([route[i, 0:NP, :] for i in members], axis=1)
        shares = jnp.concatenate([route[i, NP : 2 * NP, :] for i in members], axis=1)
        pick = jnp.logical_and(dot(expand, ranks.astype(BF16)) == want, block_ok)
        picks[g] = jnp.where(pick, 1.0, 0.0).astype(BF16)
        hi = shares.astype(BF16)
        lo = (shares - hi.astype(F32)).astype(BF16)
        for part, val in ((0, hi), (1, lo)):
            full = jnp.where(pick, dot(expand, val), 0.0)
            wcomb[g, part] = jnp.transpose(full).astype(BF16)

    state = res_ref[...].astype(F32) + prs[d].astype(F32)
    for side in range(2):
        pr[2 + side].wait_recv()
        state = state + prr[side].astype(F32)
    hid[...] = state
    rows[pl.ds(0, n_rows), :] = normalize(state, mgain_ref[...]).astype(BF16)

    far = nz // 2
    hr = n_rows // 2
    za = {}

    def hop(side, k):
        off_here = ((nz - (k - 1)) if side == 0 else (k - 1)) % nz
        off_there = (nz - k) if side == 0 else k
        src0 = pos[off_here] * n_rows
        dst0 = pos[off_there] * n_rows
        size = n_rows
        if k == far:
            size = hr
            src0 += side * hr
            dst0 += side * hr
        za[side, k] = remote(
            rows.at[pl.ds(src0, size), :],
            rows.at[pl.ds(dst0, size), :],
            za_s.at[1 + side, k],
            za_r.at[1 + side, k],
            line(1 if side == 0 else nz - 1),
        )

    def relay(k):
        for side in range(2):
            za[side, k].wait_recv()
            if k < far:
                hop(side, k + 1)

    for side in range(2):
        hop(side, 1)

    hf = kf // 2
    gu_f = {}
    wd_c = {}
    wd_f = {}

    def gu_forward():
        for m in range(2):
            for side in range(2):
                gu_c[m, side, side, 0].wait_recv()
        for i, (c0, cn) in enumerate(parts):
            for m in range(2):
                dst = gu[m][1]
                for side, frm, to in ((0, left, right), (1, right, left)):
                    at = pl.ds(frm * kd + side * half, half)
                    gu_f[m, side, i] = remote(
                        dst.at[at, pl.ds(c0, cn)],
                        dst.at[at, pl.ds(c0, cn)],
                        gu_s.at[m, side, 4 + i],
                        gu_r.at[m, side, 4 + i],
                        (to, e),
                    )

    def wd_start(n, goes_on):
        cols = pl.ds(STARTS[n], WIDTHS[n])
        for side, to in ((0, right), (1, left)):
            h = side if goes_on else 1 - side
            wd_c[n, side, h] = remote(
                wd_ref.at[pl.ds(h * hf, hf), cols],
                wdf.at[pl.ds(d * kf + h * hf, hf), cols],
                wd_s.at[n, side, h],
                wd_r.at[n, side, h],
                (to, e),
            )

    def wd_forward(n):
        cols = pl.ds(STARTS[n], WIDTHS[n])
        for side, frm, to in ((0, left, right), (1, right, left)):
            wd_c[n, side, side].wait_recv()
            at = pl.ds(frm * kf + side * hf, hf)
            wd_f[n, side] = remote(
                wdf.at[at, cols], wdf.at[at, cols], wd_s.at[n, side, 2], wd_r.at[n, side, 2], (to, e)
            )

    def wd_next(n):
        if n < CHUNKS:
            wd_forward(n)
            wd_start(n, False)
        if n + 2 < CHUNKS:
            wd_start(n + 2, True)

    ya = {}

    def dispatch(g):
        base = g * per * n_rows

        def tile(i, carry):
            cols = pl.ds(pl.multiple_of(i * 512, 512), 512)
            snd[g, :, cols] = dot(picks[g], rows[pl.ds(base, per * n_rows), cols]).astype(BF16)
            return carry

        lax.fori_loop(0, width // 512, tile, 0)
        for j in (4, 5, 3, 2, 6, 7, 1):
            t = lax.rem(p + j, NP)
            ya[g, j] = remote(
                snd.at[g, pl.ds(t * seg, seg), :],
                xin.at[g, pl.ds(p * seg, seg), :],
                ya_s.at[g, j],
                ya_r.at[g, j],
                plane(j),
            )
        mine = pltpu.make_async_copy(
            snd.at[g, pl.ds(p * seg, seg), :], xin.at[g, pl.ds(p * seg, seg), :], ya_s.at[g, 0]
        )
        mine.start()
        ya[g, 0] = mine

    for k in range(1, far // 2 + 1):
        relay(k)
    dispatch(0)
    relay(far // 2 + 1)
    gu_forward()
    for k in range(far // 2 + 2, far + 1):
        relay(k)
    dispatch(1)
    wd_start(0, True)
    wd_start(1, True)
    for m in range(2):
        local[m].wait()
    for side in range(2):
        gu_c[0, side, 1 - side, 2].wait_recv()
    for m in range(2):
        for side in range(2):
            gu_c[m, side, 1 - side, 0].wait_recv()

    def up_tile(g, cols):
        xs = xin[g]
        gate = dot(xs, wgf[:, cols])
        up = dot(xs, wuf[:, cols])
        mid[g, :, cols] = (gate / (1.0 + jnp.exp(-gate)) * up).astype(BF16)

    for i, (c0, cn) in enumerate(parts):
        for m in range(2):
            for side in range(2):
                gu_f[m, side, i].wait_recv()
        for g in range(groups):
            if i == 0:
                for j in range(1, NP):
                    ya[g, j].wait_recv()
                ya[g, 0].wait()

            def step(t, carry, g=g, c0=c0):
                up_tile(g, pl.ds(pl.multiple_of(c0 + t * 256, 256), 256))
                return carry

            lax.fori_loop(0, cn // 256, step, 0)
            if cn % 256:
                up_tile(g, pl.ds(c0 + cn // 256 * 256, cn % 256))

    ry = {}
    rz = {}
    rd = {}

    def down(n):
        def tile(g, c0, cn):
            cols = pl.ds(c0, cn)
            yout[g, :, cols] = dot(mid[g], wdf[:, cols]).astype(BF16)

        for g in range(groups):
            for c in range(0, WIDTHS[n], 256):
                tile(g, STARTS[n] + c, min(256, WIDTHS[n] - c))
        cols = pl.ds(STARTS[n], WIDTHS[n])
        for j in (4, 5, 3, 2, 6, 7, 1):
            t = lax.rem(p + j, NP)
            ry[n, j] = remote(
                yout.at[:, pl.ds(t * seg, seg), cols],
                ans.at[:, pl.ds(p * seg, seg), cols],
                ry_s.at[n, j],
                ry_r.at[n, j],
                plane(j),
            )
        mine = pltpu.make_async_copy(
            yout.at[:, pl.ds(p * seg, seg), cols],
            ans.at[:, pl.ds(p * seg, seg), cols],
            ry_s.at[n, 0],
        )
        mine.start()
        ry[n, 0] = mine

    def combine(n):
        cols = pl.ds(STARTS[n], WIDTHS[n])
        for j in range(1, NP):
            ry[n, j].wait_recv()
        ry[n, 0].wait()
        for g in (1, 0):
            part = dot(wcomb[g, 0], ans[g, :, cols]) + dot(wcomb[g, 1], ans[g, :, cols])
            psnd[g * per * n_rows : (g + 1) * per * n_rows, cols] = part.astype(BF16)
        if n == CHUNKS - 1:
            for i in range(nz - 1, 0, -1):
                off = order[i]
                slot = pos[nz - off]
                rd[slot] = remote(
                    psnd.at[pl.ds(i * n_rows, n_rows), cols],
                    partc.at[pl.ds(slot * n_rows, n_rows), :],
                    rd_s.at[i],
                    rd_r.at[slot],
                    line(off),
                )
            return
        for side in range(2):
            to = line(2 if side == 0 else nz - 2)
            near = pos[3 if side == 0 else nz - 3] * n_rows
            last = pos[far] * n_rows + side * hr
            for i, (src, dst, size) in enumerate(((last, n_rows, hr), (near, 0, n_rows))):
                rz[n, side, i] = remote(
                    psnd.at[pl.ds(src, size), cols],
                    parta.at[side, pl.ds(dst, size), cols],
                    rz_s.at[n, side, i],
                    rz_r.at[n, side, i],
                    to,
                )

    def spread(n):
        cols = pl.ds(STARTS[n], WIDTHS[n])
        for side in range(2):
            rz[n, side, 0].wait_recv()
            rz[n, side, 1].wait_recv()
            one = pos[1 if side == 0 else nz - 1] * n_rows
            two = pos[2 if side == 0 else nz - 2] * n_rows
            for r0, size, got in ((one, n_rows, 0), (two + side * hr, hr, n_rows)):
                psnd[r0 : r0 + size, cols] = (
                    psnd[r0 : r0 + size, cols].astype(F32)
                    + parta[side, got : got + size, cols].astype(F32)
                ).astype(BF16)
            for i, (src, dst, steps) in enumerate(((two, n_rows, 2), (one, 0, 1))):
                rz[n, side, 2 + i] = remote(
                    psnd.at[pl.ds(src, n_rows), cols],
                    partb.at[side, pl.ds(dst, n_rows), cols],
                    rz_s.at[n, side, 2 + i],
                    rz_r.at[n, side, 2 + i],
                    line(steps if side == 0 else nz - steps),
                )

    def gather_home(n):
        cols = slice(STARTS[n], STARTS[n] + WIDTHS[n])
        total = psnd[0:n_rows, cols].astype(F32)
        for slot in range(1, nz if n == CHUNKS - 1 else 0):
            rd[slot].wait_recv()
            total = total + partc[slot * n_rows : (slot + 1) * n_rows, :].astype(F32)
        for side in range(2 if n < CHUNKS - 1 else 0):
            for i, r0 in ((1, 0), (0, n_rows)):
                rz[n, side, 2 + i].wait_recv()
                total = total + partb[side, r0 : r0 + n_rows, cols].astype(F32)
        comb[:, cols] = hid[:, cols] + total

    wd_next(0)
    wd_next(1)
    local[2].wait()
    marks = []

    def drain(count):
        for c in sends[:count]:
            if c is not None:
                c.wait_send()
        sends[:count] = [None] * count

    for n in range(CHUNKS):
        marks.append(len(sends))
        for side in range(2):
            wd_c[n, side, 1 - side].wait_recv()
            wd_f[n, side].wait_recv()
        down(n)
        if n >= 2:
            combine(n - 1)
        wd_next(n + 2)
        if n == 0:
            combine(0)
        if n >= 2:
            spread(n - 2)
        if n >= 4:
            gather_home(n - 4)
        if n >= 1:
            drain(marks[n - 1])
    drain(marks[CHUNKS - 1])
    combine(CHUNKS - 1)
    spread(CHUNKS - 2)
    gather_home(CHUNKS - 4)
    gather_home(CHUNKS - 3)
    gather_home(CHUNKS - 2)
    gather_home(CHUNKS - 1)
    out_ref[...] = normalize(comb[...], gain_ref[...]).astype(BF16)
    drain(len(sends))


def shards(
    queries,
    kv_pool,
    page_table,
    ctx_lens,
    w_out,
    residual,
    moe_gain,
    expert_ids,
    route_weights,
    w_gate,
    w_up,
    w_down,
    final_gain,
):
    nd = lax.axis_size("dp")
    experts = lax.axis_size("expert")
    nz = experts // NP
    order = [0]
    for k in range(1, nz // 2 + 1):
        order.append(k)
        if nz - k != k:
            order.append(nz - k)
    n_rows, width = residual.shape
    group_rows, feats = queries.shape
    _, pool, page, _ = kv_pool.shape
    span = page_table.shape[1] * page
    wc = w_out.shape[1]
    kd, ff = w_gate.shape[1:]
    kf = w_down.shape[1]
    per = nz // 2
    seg = per * CAP
    gsz = NP * seg
    vmem = pl.BlockSpec(memory_space=pltpu.VMEM)
    smem = pl.BlockSpec(memory_space=pltpu.SMEM)
    hbm = pl.BlockSpec(memory_space=pl.ANY)
    dma = pltpu.SemaphoreType.DMA
    return pl.pallas_call(
        functools.partial(moe_kernel, (nd, nz, order)),
        out_shape=jax.ShapeDtypeStruct((n_rows, width), BF16),
        in_specs=[smem, vmem, hbm, vmem, vmem, vmem, vmem, vmem, vmem, hbm, hbm, hbm, vmem],
        out_specs=vmem,
        scratch_shapes=[
            pltpu.VMEM((2, pool, page, feats), BF16),
            pltpu.VMEM((group_rows, 128), jnp.int32),
            pltpu.VMEM((span, feats), BF16),
            pltpu.VMEM((span, feats), BF16),
            pltpu.VMEM((group_rows, feats), BF16),
            pltpu.VMEM((nz, NP, wc, feats), BF16),
            pltpu.VMEM((nd, n_rows, width), BF16),
            pltpu.VMEM((nd, n_rows, width), BF16),
            pltpu.VMEM((n_rows, width), F32),
            pltpu.VMEM((nd * kd, ff), BF16),
            pltpu.VMEM((nd * kd, ff), BF16),
            pltpu.VMEM((nd * kf, width), BF16),
            pltpu.VMEM((nz * n_rows, width), BF16),
            pltpu.VMEM((nz, 2 * NP, n_rows), F32),
            pltpu.VMEM((nz, 2 * NP, n_rows), F32),
            pltpu.VMEM((2, gsz, width), BF16),
            pltpu.VMEM((2, gsz, width), BF16),
            pltpu.VMEM((2, gsz, ff), BF16),
            pltpu.VMEM((2, gsz, width), BF16),
            pltpu.VMEM((2, gsz, width), BF16),
            pltpu.VMEM((2, gsz, per * n_rows), BF16),
            pltpu.VMEM((2, 2, per * n_rows, gsz), BF16),
            pltpu.VMEM((nz * n_rows, width), BF16),
            pltpu.VMEM((2, n_rows + n_rows // 2, width), BF16),
            pltpu.VMEM((2, 2 * n_rows, width), BF16),
            pltpu.VMEM((nz * n_rows, WIDTHS[-1]), BF16),
            pltpu.VMEM((n_rows, width), F32),
            dma((5,)),
            dma((nz,)),
            dma((nz,)),
            dma((NP // 2,)),
            dma((NP // 2,)),
            dma((NP // 2,)),
            dma((NP // 2,)),
            dma((nd,)),
            dma((nd,)),
            dma((2, 2, 7)),
            dma((2, 2, 7)),
            dma((CHUNKS, 2, 3)),
            dma((CHUNKS, 2, 3)),
            dma((3, nz)),
            dma((3, nz)),
            dma((2, NP)),
            dma((2, NP)),
            dma((CHUNKS, NP)),
            dma((CHUNKS, NP)),
            dma((CHUNKS, 2, 4)),
            dma((CHUNKS, 2, 4)),
            dma((nz,)),
            dma((nz,)),
        ],
        compiler_params=pltpu.CompilerParams(
            collective_id=0, has_side_effects=True, vmem_limit_bytes=62 << 20
        ),
    )(
        page_table,
        queries,
        kv_pool,
        ctx_lens[None, :],
        w_out.T,
        residual,
        moe_gain[None, :],
        expert_ids.T,
        route_weights.T,
        w_gate[0],
        w_up[0],
        w_down[0],
        final_gain[None, :],
    )


def solution(mesh):
    return jax.shard_map(
        shards,
        mesh=mesh,
        in_specs=(
            P("expert", "dp"),
            P(None, "expert", None, "dp"),
            P("expert", None),
            P("expert"),
            P("dp", "expert"),
            P(("expert", "dp"), None),
            P(),
            P(("expert", "dp"), None),
            P(("expert", "dp"), None),
            P("expert", "dp", None),
            P("expert", "dp", None),
            P("expert", "dp", None),
            P(),
        ),
        out_specs=P(("expert", "dp"), None),
        check_vma=False,
    )
```

```python
import functools
import math

import jax
import jax.numpy as jnp
from jax import lax
from jax.experimental import pallas as pl
from jax.experimental.pallas import tpu as pltpu
from jax.sharding import PartitionSpec as P

HD = 128
TOP = 6
CAP = 12
NP = 8
WIDTHS = (256, 384, 384, 384, 256, 256, 128)
STARTS = (0, 256, 640, 1024, 1408, 1664, 1920)
CHUNKS = 7
MESH = pl.DeviceIdType.MESH
F32 = jnp.float32
BF16 = jnp.bfloat16


def normalize(values, gain):
    mean_sq = jnp.mean(values * values, axis=-1, keepdims=True)
    return values * lax.rsqrt(mean_sq + 1e-06) * gain


def iota(shape, axis):
    return lax.broadcasted_iota(jnp.int32, shape, axis)


def dot(a, b):
    return jnp.dot(a, b, preferred_element_type=F32)


def moe_kernel(
    sizes,
    table_ref,
    q_hbm,
    kv_ref,
    lens_ref,
    wot_ref,
    res_hbm,
    mgain_ref,
    ids_ref,
    rw_ref,
    wg_ref,
    wu_ref,
    wd_ref,
    gain_ref,
    out_ref,
    q_ref,
    res_ref,
    kvs,
    lens_t,
    keys,
    vals,
    ctx,
    wo,
    prs,
    prr,
    hid,
    wgf,
    wuf,
    wdf,
    rows,
    route_out,
    route,
    snd,
    xin,
    mid,
    yout,
    ans,
    picks,
    wcomb,
    psnd,
    parta,
    partb,
    partc,
    comb,
    loc_sem,
    w1_s,
    w1_r,
    w2_s,
    w2_r,
    w3_s,
    w3_r,
    pr_s,
    pr_r,
    gu_s,
    gu_r,
    wd_s,
    wd_r,
    za_s,
    za_r,
    ya_s,
    ya_r,
    ry_s,
    ry_r,
    rz_s,
    rz_r,
    rd_s,
    rd_r,
):
    nd, nz, order = sizes
    pos = {off: i for i, off in enumerate(order)}
    groups = 2
    per = nz // groups
    d = lax.axis_index("dp")
    e = lax.axis_index("expert")
    z = e // NP
    p = lax.rem(e, NP)
    n_rows, width = res_ref.shape
    kd = wg_ref.shape[0]
    ff = wg_ref.shape[1]
    kf = wd_ref.shape[0]
    seg = per * CAP
    gsz = NP * seg
    right = lax.rem(d + 1, nd)
    left = lax.rem(d + nd - 1, nd)
    sends = []

    def plane(j):
        return (d, z * NP + lax.rem(p + j, NP))

    def line(off):
        return (d, lax.rem(z + off, nz) * NP + p)

    def remote(src, dst, s, r, to):
        c = pltpu.make_async_remote_copy(
            src_ref=src, dst_ref=dst, send_sem=s, recv_sem=r, device_id=to, device_id_type=MESH
        )
        c.start()
        sends.append(c)
        return c

    kv_c = pltpu.make_async_copy(kv_ref, kvs, loc_sem.at[4])
    kv_c.start()
    q_c = pltpu.make_async_copy(q_hbm, q_ref, loc_sem.at[5])
    q_c.start()
    res_c = pltpu.make_async_copy(res_hbm, res_ref, loc_sem.at[6])
    res_c.start()
    barrier = pltpu.get_barrier_semaphore()
    peers = [(right, e), (left, e)]
    peers += [line(o) for o in range(1, nz)] + [plane(j) for j in range(1, NP)]
    for peer in peers:
        pl.semaphore_signal(barrier, inc=1, device_id=peer, device_id_type=MESH)
    wo[z, p] = wot_ref[...]
    pl.semaphore_wait(barrier, len(peers))

    gu = [(wg_ref, wgf), (wu_ref, wuf)]
    half = kd // 2
    gu_c = {}

    parts = ((0, 512), (512, 512), (1024, ff - 1024))
    cut = 6 * 128

    def ring_start(m, goes_on, i=0, c0=0, cn=ff):
        src, dst = gu[m]
        for side, to in ((0, right), (1, left)):
            h = side if goes_on else 1 - side
            gu_c[m, side, h, i] = remote(
                src.at[pl.ds(h * half, half), pl.ds(c0, cn)],
                dst.at[pl.ds(d * kd + h * half, half), pl.ds(c0, cn)],
                gu_s.at[m, side, h + i],
                gu_r.at[m, side, h + i],
                (to, e),
            )

    ring_start(0, True)

    w1 = {}
    for off in order[1:]:
        w1[off] = remote(wot_ref, wo.at[z, p], w1_s.at[off], w1_r.at[off], line(off))
    ring_start(0, False, 0, 0, cut)

    experts = nz * NP
    named = jnp.zeros((experts, n_rows), F32)
    share = jnp.zeros((experts, n_rows), F32)
    for k in range(TOP):
        hit = ids_ref[k : k + 1, :] == iota((experts, n_rows), 0)
        named = named + jnp.where(hit, 1.0, 0.0)
        share = share + jnp.where(hit, rw_ref[k : k + 1, :], 0.0)
    upper = jnp.where(iota((n_rows, n_rows), 0) < iota((n_rows, n_rows), 1), 1.0, 0.0).astype(BF16)
    rank = dot(named.astype(BF16), upper)
    rank = jnp.where(named > 0.5, rank, -1.0)
    for i in range(nz):
        route_out[i, 0:NP, :] = rank[i * NP : (i + 1) * NP, :]
        route_out[i, NP : 2 * NP, :] = share[i * NP : (i + 1) * NP, :]
    own_route = pltpu.make_async_copy(route_out.at[z], route.at[0], loc_sem.at[3])
    own_route.start()
    zr = {}
    for off in order[1:]:
        slot = pos[nz - off]
        zt = lax.rem(z + off, nz)
        zr[slot] = remote(
            route_out.at[zt], route.at[slot], za_s.at[0, off], za_r.at[0, slot], line(off)
        )

    for off in order[1:]:
        w1[off].wait_recv()
    sib = p + 1 - 2 * lax.rem(p, 2)
    sib_to = (d, z * NP + sib)
    w2 = {}
    w3 = {}
    for k in range(1, NP // 2):
        w2[k] = remote(wo.at[:, p], wo.at[:, p], w2_s.at[k], w2_r.at[k], plane(2 * k))
    w3[0] = remote(wo.at[:, p], wo.at[:, p], w3_s.at[0], w3_r.at[0], sib_to)

    seqs = table_ref.shape[0]
    pages = table_ref.shape[1]
    pool = kv_ref.shape[1]
    page = kv_ref.shape[2]
    span = pages * page
    q_rows = q_ref.shape[0] // seqs
    scale = 1.0 / math.sqrt(HD)
    lens_t[...] = jnp.transpose(jnp.broadcast_to(lens_ref[...], (128, lens_ref.shape[1])))
    kv_c.wait()
    q_c.wait()
    res_c.wait()

    def attend(s, carry):
        for i in range(pages):
            at = lax.rem(table_ref[s, i], pool)
            keys[i * page : (i + 1) * page, :] = kvs[0, at]
            vals[i * page : (i + 1) * page, :] = kvs[1, at]
        here = pl.ds(pl.multiple_of(s * q_rows, q_rows), q_rows)
        seen = iota((q_rows, span), 1) < lens_t[here, 0:1]
        for h in range(q_ref.shape[1] // HD):
            cols = slice(h * HD, (h + 1) * HD)
            sc = lax.dot_general(
                q_ref[here, cols], keys[:, cols], (((1,), (1,)), ((), ())), preferred_element_type=F32
            )
            sc = jnp.where(seen, sc * scale, -1e30)
            ex = jnp.where(seen, jnp.exp(sc - jnp.max(sc, axis=-1, keepdims=True)), 0.0)
            pr = (ex / jnp.sum(ex, axis=-1, keepdims=True)).astype(BF16)
            ctx[here, cols] = dot(pr, vals[:, cols]).astype(BF16)
        return carry

    lax.fori_loop(0, seqs, attend, 0)

    for k in range(1, NP // 2):
        w2[k].wait_recv()
        got = lax.rem(p + NP - 2 * k, NP)
        w3[k] = remote(wo.at[:, got], wo.at[:, got], w3_s.at[k], w3_r.at[k], sib_to)
    for k in range(NP // 2):
        w3[k].wait_recv()

    wn = NP * wot_ref.shape[0]

    def project(i, carry):
        w = wo[i].reshape(wn, wot_ref.shape[1])
        val = lax.dot_general(
            ctx[...], w, (((1,), (1,)), ((), ())), preferred_element_type=F32
        ).astype(BF16)
        cols = pl.ds(pl.multiple_of(i * wn, wn), wn)
        for j in range(nd):
            prs[j, :, cols] = val[j * n_rows : (j + 1) * n_rows, :]
        return carry

    lax.fori_loop(0, nz, project, 0)
    pr = {}
    hw = width // 2
    opposite = lax.rem(d + 2, nd)
    for side, to in ((0, right), (1, left)):
        cols = pl.ds(side * hw, hw)
        pr[side] = remote(
            prs.at[opposite, :, cols],
            prr.at[2, :, cols],
            pr_s.at[side],
            pr_r.at[side],
            (to, e),
        )
    ring_start(0, False, 2, cut, ff - cut)
    for side, to in ((0, right), (1, left)):
        pr[side].wait_recv()
        cols = slice(side * hw, (side + 1) * hw)
        prs[to, :, cols] = (prs[to, :, cols].astype(F32) + prr[2, :, cols].astype(F32)).astype(BF16)
        pr[2 + side] = remote(
            prs.at[to], prr.at[side], pr_s.at[2 + side], pr_r.at[2 + side], (to, e)
        )
    ring_start(1, True)
    ring_start(1, False)
    local = []
    for m, (src, dst) in enumerate(gu):
        c = pltpu.make_async_copy(src, dst.at[pl.ds(d * kd, kd), :], loc_sem.at[m])
        c.start()
        local.append(c)
    c = pltpu.make_async_copy(wd_ref, wdf.at[pl.ds(d * kf, kf), :], loc_sem.at[2])
    c.start()
    local.append(c)

    slot_i = iota((gsz, per * n_rows), 0)
    expand = jnp.where(iota((gsz, NP), 0) // seg == iota((gsz, NP), 1), 1.0, 0.0).astype(BF16)
    want = lax.rem(slot_i, CAP).astype(F32)
    block_ok = lax.rem(slot_i, seg) // CAP == iota((gsz, per * n_rows), 1) // n_rows
    for g in range(groups):
        members = range(g * per, (g + 1) * per)
        for i in members:
            if i == 0:
                own_route.wait()
            else:
                zr[i].wait_recv()
        ranks = jnp.concatenate([route[i, 0:NP, :] for i in members], axis=1)
        shares = jnp.concatenate([route[i, NP : 2 * NP, :] for i in members], axis=1)
        pick = jnp.logical_and(dot(expand, ranks.astype(BF16)) == want, block_ok)
        picks[g] = jnp.where(pick, 1.0, 0.0).astype(BF16)
        hi = shares.astype(BF16)
        lo = (shares - hi.astype(F32)).astype(BF16)
        for part, val in ((0, hi), (1, lo)):
            full = jnp.where(pick, dot(expand, val), 0.0)
            wcomb[g, part] = jnp.transpose(full).astype(BF16)

    state = res_ref[...].astype(F32) + prs[d].astype(F32)
    for side in range(2):
        pr[2 + side].wait_recv()
        state = state + prr[side].astype(F32)
    hid[...] = state
    rows[pl.ds(0, n_rows), :] = normalize(state, mgain_ref[...]).astype(BF16)

    far = nz // 2
    hr = n_rows // 2
    za = {}

    def hop(side, k):
        off_here = ((nz - (k - 1)) if side == 0 else (k - 1)) % nz
        off_there = (nz - k) if side == 0 else k
        src0 = pos[off_here] * n_rows
        dst0 = pos[off_there] * n_rows
        size = n_rows
        if k == far:
            size = hr
            src0 += side * hr
            dst0 += side * hr
        za[side, k] = remote(
            rows.at[pl.ds(src0, size), :],
            rows.at[pl.ds(dst0, size), :],
            za_s.at[1 + side, k],
            za_r.at[1 + side, k],
            line(1 if side == 0 else nz - 1),
        )

    def relay(k):
        for side in range(2):
            za[side, k].wait_recv()
            if k < far:
                hop(side, k + 1)

    for side in range(2):
        hop(side, 1)

    hf = kf // 2
    gu_f = {}
    wd_c = {}
    wd_f = {}

    def gu_forward():
        for m in range(2):
            for side in range(2):
                gu_c[m, side, side, 0].wait_recv()
        for i, (c0, cn) in enumerate(parts):
            for m in range(2):
                dst = gu[m][1]
                for side, frm, to in ((0, left, right), (1, right, left)):
                    at = pl.ds(frm * kd + side * half, half)
                    gu_f[m, side, i] = remote(
                        dst.at[at, pl.ds(c0, cn)],
                        dst.at[at, pl.ds(c0, cn)],
                        gu_s.at[m, side, 4 + i],
                        gu_r.at[m, side, 4 + i],
                        (to, e),
                    )

    def wd_start(n, goes_on):
        cols = pl.ds(STARTS[n], WIDTHS[n])
        for side, to in ((0, right), (1, left)):
            h = side if goes_on else 1 - side
            wd_c[n, side, h] = remote(
                wd_ref.at[pl.ds(h * hf, hf), cols],
                wdf.at[pl.ds(d * kf + h * hf, hf), cols],
                wd_s.at[n, side, h],
                wd_r.at[n, side, h],
                (to, e),
            )

    def wd_forward(n):
        cols = pl.ds(STARTS[n], WIDTHS[n])
        for side, frm, to in ((0, left, right), (1, right, left)):
            wd_c[n, side, side].wait_recv()
            at = pl.ds(frm * kf + side * hf, hf)
            wd_f[n, side] = remote(
                wdf.at[at, cols], wdf.at[at, cols], wd_s.at[n, side, 2], wd_r.at[n, side, 2], (to, e)
            )

    def wd_next(n):
        if n < CHUNKS:
            wd_forward(n)
            wd_start(n, False)
        if n + 2 < CHUNKS:
            wd_start(n + 2, True)

    ya = {}

    def dispatch(g):
        base = g * per * n_rows

        def tile(i, carry):
            cols = pl.ds(pl.multiple_of(i * 512, 512), 512)
            snd[g, :, cols] = dot(picks[g], rows[pl.ds(base, per * n_rows), cols]).astype(BF16)
            return carry

        lax.fori_loop(0, width // 512, tile, 0)
        for j in (4, 5, 3, 2, 6, 7, 1):
            t = lax.rem(p + j, NP)
            ya[g, j] = remote(
                snd.at[g, pl.ds(t * seg, seg), :],
                xin.at[g, pl.ds(p * seg, seg), :],
                ya_s.at[g, j],
                ya_r.at[g, j],
                plane(j),
            )
        mine = pltpu.make_async_copy(
            snd.at[g, pl.ds(p * seg, seg), :], xin.at[g, pl.ds(p * seg, seg), :], ya_s.at[g, 0]
        )
        mine.start()
        ya[g, 0] = mine

    for k in range(1, far // 2 + 1):
        relay(k)
    dispatch(0)
    relay(far // 2 + 1)
    gu_forward()
    for k in range(far // 2 + 2, far + 1):
        relay(k)
    dispatch(1)
    wd_start(0, True)
    wd_start(1, True)
    for m in range(2):
        local[m].wait()
    for side in range(2):
        gu_c[0, side, 1 - side, 2].wait_recv()
    for m in range(2):
        for side in range(2):
            gu_c[m, side, 1 - side, 0].wait_recv()

    def up_tile(g, cols):
        xs = xin[g]
        gate = dot(xs, wgf[:, cols])
        up = dot(xs, wuf[:, cols])
        mid[g, :, cols] = (gate / (1.0 + jnp.exp(-gate)) * up).astype(BF16)

    for i, (c0, cn) in enumerate(parts):
        for m in range(2):
            for side in range(2):
                gu_f[m, side, i].wait_recv()
        for g in range(groups):
            if i == 0:
                for j in range(1, NP):
                    ya[g, j].wait_recv()
                ya[g, 0].wait()

            def step(t, carry, g=g, c0=c0):
                up_tile(g, pl.ds(pl.multiple_of(c0 + t * 256, 256), 256))
                return carry

            lax.fori_loop(0, cn // 256, step, 0)
            if cn % 256:
                up_tile(g, pl.ds(c0 + cn // 256 * 256, cn % 256))

    ry = {}
    rz = {}
    rd = {}

    def down(n):
        def tile(g, c0, cn):
            cols = pl.ds(c0, cn)
            yout[g, :, cols] = dot(mid[g], wdf[:, cols]).astype(BF16)

        for g in range(groups):
            for c in range(0, WIDTHS[n], 256):
                tile(g, STARTS[n] + c, min(256, WIDTHS[n] - c))
        cols = pl.ds(STARTS[n], WIDTHS[n])
        for j in (4, 5, 3, 2, 6, 7, 1):
            t = lax.rem(p + j, NP)
            ry[n, j] = remote(
                yout.at[:, pl.ds(t * seg, seg), cols],
                ans.at[:, pl.ds(p * seg, seg), cols],
                ry_s.at[n, j],
                ry_r.at[n, j],
                plane(j),
            )
        mine = pltpu.make_async_copy(
            yout.at[:, pl.ds(p * seg, seg), cols],
            ans.at[:, pl.ds(p * seg, seg), cols],
            ry_s.at[n, 0],
        )
        mine.start()
        ry[n, 0] = mine

    def combine(n):
        cols = pl.ds(STARTS[n], WIDTHS[n])
        for j in range(1, NP):
            ry[n, j].wait_recv()
        ry[n, 0].wait()
        for g in (1, 0):
            part = dot(wcomb[g, 0], ans[g, :, cols]) + dot(wcomb[g, 1], ans[g, :, cols])
            psnd[g * per * n_rows : (g + 1) * per * n_rows, cols] = part.astype(BF16)
        if n == CHUNKS - 1:
            for i in range(nz - 1, 0, -1):
                off = order[i]
                slot = pos[nz - off]
                rd[slot] = remote(
                    psnd.at[pl.ds(i * n_rows, n_rows), cols],
                    partc.at[pl.ds(slot * n_rows, n_rows), :],
                    rd_s.at[i],
                    rd_r.at[slot],
                    line(off),
                )
            return
        for side in range(2):
            to = line(2 if side == 0 else nz - 2)
            near = pos[3 if side == 0 else nz - 3] * n_rows
            last = pos[far] * n_rows + side * hr
            for i, (src, dst, size) in enumerate(((last, n_rows, hr), (near, 0, n_rows))):
                rz[n, side, i] = remote(
                    psnd.at[pl.ds(src, size), cols],
                    parta.at[side, pl.ds(dst, size), cols],
                    rz_s.at[n, side, i],
                    rz_r.at[n, side, i],
                    to,
                )

    def spread(n):
        cols = pl.ds(STARTS[n], WIDTHS[n])
        for side in range(2):
            rz[n, side, 0].wait_recv()
            rz[n, side, 1].wait_recv()
            one = pos[1 if side == 0 else nz - 1] * n_rows
            two = pos[2 if side == 0 else nz - 2] * n_rows
            for r0, size, got in ((one, n_rows, 0), (two + side * hr, hr, n_rows)):
                psnd[r0 : r0 + size, cols] = (
                    psnd[r0 : r0 + size, cols].astype(F32)
                    + parta[side, got : got + size, cols].astype(F32)
                ).astype(BF16)
            for i, (src, dst, steps) in enumerate(((two, n_rows, 2), (one, 0, 1))):
                rz[n, side, 2 + i] = remote(
                    psnd.at[pl.ds(src, n_rows), cols],
                    partb.at[side, pl.ds(dst, n_rows), cols],
                    rz_s.at[n, side, 2 + i],
                    rz_r.at[n, side, 2 + i],
                    line(steps if side == 0 else nz - steps),
                )

    def gather_home(n):
        cols = slice(STARTS[n], STARTS[n] + WIDTHS[n])
        total = psnd[0:n_rows, cols].astype(F32)
        for slot in range(1, nz if n == CHUNKS - 1 else 0):
            rd[slot].wait_recv()
            total = total + partc[slot * n_rows : (slot + 1) * n_rows, :].astype(F32)
        for side in range(2 if n < CHUNKS - 1 else 0):
            for i, r0 in ((1, 0), (0, n_rows)):
                rz[n, side, 2 + i].wait_recv()
                total = total + partb[side, r0 : r0 + n_rows, cols].astype(F32)
        comb[:, cols] = hid[:, cols] + total

    wd_next(0)
    wd_next(1)
    local[2].wait()
    marks = []

    def drain(count):
        for c in sends[:count]:
            if c is not None:
                c.wait_send()
        sends[:count] = [None] * count

    for n in range(CHUNKS):
        marks.append(len(sends))
        for side in range(2):
            wd_c[n, side, 1 - side].wait_recv()
            wd_f[n, side].wait_recv()
        down(n)
        if n >= 2:
            combine(n - 1)
        wd_next(n + 2)
        if n == 0:
            combine(0)
        if n >= 2:
            spread(n - 2)
        if n >= 4:
            gather_home(n - 4)
        if n >= 1:
            drain(marks[n - 1])
    drain(marks[CHUNKS - 1])
    gather_home(CHUNKS - 4)
    combine(CHUNKS - 1)
    spread(CHUNKS - 2)
    gather_home(CHUNKS - 3)
    gather_home(CHUNKS - 2)
    gather_home(CHUNKS - 1)
    out_ref[...] = normalize(comb[...], gain_ref[...]).astype(BF16)
    drain(len(sends))


def shards(
    queries,
    kv_pool,
    page_table,
    ctx_lens,
    w_out,
    residual,
    moe_gain,
    expert_ids,
    route_weights,
    w_gate,
    w_up,
    w_down,
    final_gain,
):
    nd = lax.axis_size("dp")
    experts = lax.axis_size("expert")
    nz = experts // NP
    order = [0]
    for k in range(1, nz // 2 + 1):
        order.append(k)
        if nz - k != k:
            order.append(nz - k)
    n_rows, width = residual.shape
    group_rows, feats = queries.shape
    _, pool, page, _ = kv_pool.shape
    span = page_table.shape[1] * page
    wc = w_out.shape[1]
    kd, ff = w_gate.shape[1:]
    kf = w_down.shape[1]
    per = nz // 2
    seg = per * CAP
    gsz = NP * seg
    vmem = pl.BlockSpec(memory_space=pltpu.VMEM)
    smem = pl.BlockSpec(memory_space=pltpu.SMEM)
    hbm = pl.BlockSpec(memory_space=pl.ANY)
    dma = pltpu.SemaphoreType.DMA
    return pl.pallas_call(
        functools.partial(moe_kernel, (nd, nz, order)),
        out_shape=jax.ShapeDtypeStruct((n_rows, width), BF16),
        in_specs=[smem, hbm, hbm, vmem, vmem, hbm, vmem, vmem, vmem, hbm, hbm, hbm, vmem],
        out_specs=vmem,
        scratch_shapes=[
            pltpu.VMEM((group_rows, feats), BF16),
            pltpu.VMEM((n_rows, width), BF16),
            pltpu.VMEM((2, pool, page, feats), BF16),
            pltpu.VMEM((group_rows, 128), jnp.int32),
            pltpu.VMEM((span, feats), BF16),
            pltpu.VMEM((span, feats), BF16),
            pltpu.VMEM((group_rows, feats), BF16),
            pltpu.VMEM((nz, NP, wc, feats), BF16),
            pltpu.VMEM((nd, n_rows, width), BF16),
            pltpu.VMEM((nd, n_rows, width), BF16),
            pltpu.VMEM((n_rows, width), F32),
            pltpu.VMEM((nd * kd, ff), BF16),
            pltpu.VMEM((nd * kd, ff), BF16),
            pltpu.VMEM((nd * kf, width), BF16),
            pltpu.VMEM((nz * n_rows, width), BF16),
            pltpu.VMEM((nz, 2 * NP, n_rows), F32),
            pltpu.VMEM((nz, 2 * NP, n_rows), F32),
            pltpu.VMEM((2, gsz, width), BF16),
            pltpu.VMEM((2, gsz, width), BF16),
            pltpu.VMEM((2, gsz, ff), BF16),
            pltpu.VMEM((2, gsz, width), BF16),
            pltpu.VMEM((2, gsz, width), BF16),
            pltpu.VMEM((2, gsz, per * n_rows), BF16),
            pltpu.VMEM((2, 2, per * n_rows, gsz), BF16),
            pltpu.VMEM((nz * n_rows, width), BF16),
            pltpu.VMEM((2, n_rows + n_rows // 2, width), BF16),
            pltpu.VMEM((2, 2 * n_rows, width), BF16),
            pltpu.VMEM((nz * n_rows, WIDTHS[-1]), BF16),
            pltpu.VMEM((n_rows, width), F32),
            dma((7,)),
            dma((nz,)),
            dma((nz,)),
            dma((NP // 2,)),
            dma((NP // 2,)),
            dma((NP // 2,)),
            dma((NP // 2,)),
            dma((nd,)),
            dma((nd,)),
            dma((2, 2, 7)),
            dma((2, 2, 7)),
            dma((CHUNKS, 2, 3)),
            dma((CHUNKS, 2, 3)),
            dma((3, nz)),
            dma((3, nz)),
            dma((2, NP)),
            dma((2, NP)),
            dma((CHUNKS, NP)),
            dma((CHUNKS, NP)),
            dma((CHUNKS, 2, 4)),
            dma((CHUNKS, 2, 4)),
            dma((nz,)),
            dma((nz,)),
        ],
        compiler_params=pltpu.CompilerParams(
            collective_id=0, has_side_effects=True, vmem_limit_bytes=62 << 20
        ),
    )(
        page_table,
        queries,
        kv_pool,
        ctx_lens[None, :],
        w_out.T,
        residual,
        moe_gain[None, :],
        expert_ids.T,
        route_weights.T,
        w_gate[0],
        w_up[0],
        w_down[0],
        final_gain[None, :],
    )


def solution(mesh):
    return jax.shard_map(
        shards,
        mesh=mesh,
        in_specs=(
            P("expert", "dp"),
            P(None, "expert", None, "dp"),
            P("expert", None),
            P("expert"),
            P("dp", "expert"),
            P(("expert", "dp"), None),
            P(),
            P(("expert", "dp"), None),
            P(("expert", "dp"), None),
            P("expert", "dp", None),
            P("expert", "dp", None),
            P("expert", "dp", None),
            P(),
        ),
        out_specs=P(("expert", "dp"), None),
        check_vma=False,
    )
```
